32 devices in a mesh: seq: 8 (over y, x, core), head: 4 (over z).
Axes of the slice: x: 2, y: 2, z: 4, core: 2. Of those that a mesh axis runs over, the one named last changes fastest.
Arguments:
- query_lin: bfloat16 [512, 4096], P('seq', 'head'), may hold values from -6 to 6
- key_lin: bfloat16 [512, 4096], P('seq', 'head'), may hold values from -6 to 6
- value_lin: bfloat16 [512, 4096], P('seq', 'head'), may hold values from -6 to 6
- log_decay: float32 [32, 512], P('head', 'seq'), may hold values from -1.6 to 0
- query_soft: bfloat16 [512, 4096], P(('seq', 'head')), may hold values from -4.5 to 4.5
- key_soft: bfloat16 [512, 512], P(('seq', 'head')), may hold values from -4.5 to 4.5
- value_soft: bfloat16 [512, 512], P(('seq', 'head')), may hold values from -6 to 6
- doc_start: int32 [512], P('seq'), may hold values from 0 to 480, as said below
Outputs:
- lin_out: bfloat16 [512, 4096], P('seq', 'head')
- soft_out: bfloat16 [512, 4096], P('seq', 'head')
- soft_lse: float32 [32, 512], P('head', 'seq')
The draws below stay inside these ranges and needn't reach their ends.
Inputs may be any that keep to these rules, and one draw needn't show every extreme that they name: doc_start[t] is the first position of the document that holds token t: 0 for the first document, never above t, the same over a document; at most 4 documents; every document but the first and the last starts at a position of 1 to 32; the last document starts at 480.
All inputs are finite; a program needn't handle non-finite values.
Results may differ from the reference program's by a relative error of at most 0.003.
Values may be sent and summed in bfloat16 or wider, within the bound.
A program may use at most 256 MiB of HBM per device.

```python
import math
import jax
import jax.numpy as jnp
from jax import lax

DH = 128
LINEAR_HEADS = 32
SOFT_HEADS = 32
KV_HEADS = 4
DOCS = 4
TOK_DEV = 64
TOKEN_COUNT = 512


def draw_log_decay(key, part):
    every_key_row = jax.random.split(key, 7)
    slow_count = LINEAR_HEADS // 2
    order = jax.random.permutation(every_key_row[0], LINEAR_HEADS)
    slow_heads = order < slow_count
    slow_rate = jnp.exp(jax.random.uniform(every_key_row[1], (LINEAR_HEADS,), jnp.float32, math.log(0.2 / TOKEN_COUNT), math.log(0.6 / TOKEN_COUNT)))
    fast_rate = jnp.exp(jax.random.uniform(every_key_row[2], (LINEAR_HEADS,), jnp.float32, math.log(1.0 / 200.0), math.log(1.0 / 30.0)))
    rate = jnp.where(slow_heads, slow_rate, fast_rate)
    blocks = TOKEN_COUNT // TOK_DEV
    block_factor = jnp.exp(jax.random.uniform(every_key_row[3], (LINEAR_HEADS, blocks, 1), jnp.float32, -0.7, 0.7))
    token_factor = jax.random.uniform(every_key_row[4], (LINEAR_HEADS, blocks, TOK_DEV), jnp.float32, 0.5, 1.5)
    base_offset = -(rate[:, None, None] * block_factor * token_factor).reshape(LINEAR_HEADS, TOKEN_COUNT)
    cluster_positions = jax.random.randint(every_key_row[5], (LINEAR_HEADS, 2), 0, TOKEN_COUNT)
    cluster_depth = jnp.log(jax.random.uniform(every_key_row[6], (LINEAR_HEADS, 2), jnp.float32, 0.5, 0.8))
    token_positions = jnp.arange(TOKEN_COUNT, dtype=jnp.int32)
    cluster_matches = token_positions[None, None, :] == cluster_positions[:, :, None]
    token_clusters = jnp.sum(jnp.where(cluster_matches, cluster_depth[:, :, None], 0.0), axis=1)
    return (base_offset + token_clusters).astype(jnp.float32)


def draw_doc_start(key, part):
    last_edge = TOKEN_COUNT - TOK_DEV // 2
    drawn_edges = jax.random.randint(jax.random.fold_in(key, 5), (DOCS - 2,), 1, TOK_DEV // 2 + 1)
    doc_edges = jnp.concatenate([drawn_edges.astype(jnp.int32), jnp.full((1,), last_edge, jnp.int32)])
    token_positions = jnp.arange(TOKEN_COUNT, dtype=jnp.int32)
    picked = jnp.where(doc_edges[None, :] <= token_positions[:, None], doc_edges[None, :], 0)
    return jnp.max(picked, axis=1).astype(jnp.int32)


def soft_pair(key):
    base_key = jax.random.fold_in(key, 17)
    key_key, query_key = jax.random.split(base_key, 2)
    keys_drawn = jnp.clip(jax.random.normal(key_key, (TOKEN_COUNT, KV_HEADS * DH), jnp.float32), -4.5, 4.5)
    queries_drawn = jnp.clip(jax.random.normal(query_key, (TOKEN_COUNT, SOFT_HEADS * DH), jnp.float32), -4.5, 4.5)
    return (keys_drawn, queries_drawn)


def draw_key_soft(key, part):
    return soft_pair(key)[0].astype(jnp.bfloat16)


def draw_query_soft(key, part):
    return soft_pair(key)[1].astype(jnp.bfloat16)


def block_scale(rng, extent, pieces, least, high):
    def one(axis_at, shards_of):
        heights = jax.random.uniform(jax.random.fold_in(jax.random.fold_in(rng, 6), axis_at), (shards_of,), jnp.float32, least / len(pieces), high / len(pieces))
        return jnp.repeat(jnp.exp(heights), extent[axis_at] // shards_of).reshape((-1,) + (1,) * (len(extent) - axis_at - 1))

    factor_of = one(*pieces[0])
    for cut in pieces[1:]:
        factor_of = factor_of * one(*cut)
    return factor_of


def gaussian(key, dims, spread, bound, cuts=(), held_as=jnp.bfloat16):
    result = spread * jax.random.normal(key, dims, jnp.float32)
    if cuts:
        result = result * block_scale(key, dims, cuts, -0.22, 0.18)
    return jnp.clip(result, -bound, bound).astype(held_as)


def setup_inputs(seed: int = 0) -> dict:
    key_of = jax.random.split(jax.random.key(seed), 9)
    query_lin = gaussian(key_of[0], (TOKEN_COUNT, LINEAR_HEADS * DH), 1.0, 6.0, ((0, 8), (1, 4)))
    key_lin = gaussian(key_of[1], (TOKEN_COUNT, LINEAR_HEADS * DH), 1.0, 6.0, ((0, 8), (1, 4)))
    value_lin = gaussian(key_of[2], (TOKEN_COUNT, LINEAR_HEADS * DH), 1.0, 6.0, ((0, 8), (1, 4)))
    log_decay = draw_log_decay(jax.random.fold_in(key_of[8], 71), 0)
    query_soft = draw_query_soft(jax.random.fold_in(key_of[8], 71), 0)
    key_soft = draw_key_soft(jax.random.fold_in(key_of[8], 71), 0)
    value_soft = gaussian(key_of[6], (TOKEN_COUNT, KV_HEADS * DH), 1.0, 6.0, ((0, 32),))
    doc_start = draw_doc_start(jax.random.fold_in(key_of[8], 71), 0)
    return {"query_lin": query_lin, "key_lin": key_lin, "value_lin": value_lin, "log_decay": log_decay, "query_soft": query_soft, "key_soft": key_soft, "value_soft": value_soft, "doc_start": doc_start}


HIGHEST = lax.Precision.HIGHEST

def span_terms(query_heads, key_heads, value_heads, decay_rows, doc_rows, first_place):
    span_len = query_heads.shape[0]
    cumulative = jnp.cumsum(decay_rows, axis=1)
    totals = cumulative[:, -1]
    token_positions = first_place + jnp.arange(span_len, dtype=jnp.int32)
    allowed = (token_positions[None, :] <= token_positions[:, None]) & (doc_rows[:, None] <= token_positions[None, :])
    decay_gap = jnp.where(allowed[None], cumulative[:, :, None] - cumulative[:, None, :], 0.0)
    decay_mat = jnp.where(allowed[None], jnp.exp(decay_gap), 0.0)
    query_float = query_heads.astype(jnp.float32)
    key_float = key_heads.astype(jnp.float32)
    value_float = value_heads.astype(jnp.float32)
    scores = jnp.einsum('thd,shd->hts', query_float, key_float, precision=HIGHEST)
    inner_part = jnp.einsum('hts,shd->thd', scores * decay_mat, value_float, precision=HIGHEST)
    keep_mask = (doc_rows == doc_rows[-1]).astype(jnp.float32)
    tail_weight = jnp.exp(totals[:, None] - cumulative) * keep_mask[None, :]
    weighted_keys = key_float * jnp.transpose(tail_weight)[:, :, None]
    fresh_state = jnp.einsum('shd,she->hde', weighted_keys, value_float, precision=HIGHEST)
    carry_on = (doc_rows[-1] < first_place).astype(jnp.float32)
    factor = jnp.exp(totals) * carry_on
    read_mask = (doc_rows < first_place).astype(jnp.float32)[:, None] * jnp.transpose(jnp.exp(cumulative))
    return (inner_part, fresh_state, factor, read_mask, query_float)

def lightning(query_lin, key_lin, value_lin, log_decay, doc_start):
    blocks = TOKEN_COUNT // TOK_DEV
    query_parts = query_lin.reshape(blocks, TOK_DEV, LINEAR_HEADS, DH)
    key_parts = key_lin.reshape(blocks, TOK_DEV, LINEAR_HEADS, DH)
    value_parts = value_lin.reshape(blocks, TOK_DEV, LINEAR_HEADS, DH)
    decay_parts = jnp.transpose(log_decay.reshape(LINEAR_HEADS, blocks, TOK_DEV), (1, 0, 2))
    doc_parts = doc_start.reshape(blocks, TOK_DEV)
    block_starts = jnp.arange(blocks, dtype=jnp.int32) * TOK_DEV

    def advance(carried, slices):
        query_block, key_block, value_block, decay_block, doc_block, first_place = slices
        inner_part, fresh_state, factor, read_mask, query_float = span_terms(query_block, key_block, value_block, decay_block, doc_block, first_place)
        outer_part = jnp.einsum('thd,hde->the', query_float, carried, precision=HIGHEST) * read_mask[:, :, None]
        mixed_out = inner_part + outer_part
        normed = mixed_out * lax.rsqrt(lax.optimization_barrier(jnp.mean(mixed_out * mixed_out, axis=-1, keepdims=True)) + 1e-06)
        return (factor[:, None, None] * carried + fresh_state, normed.astype(jnp.bfloat16))
    start_state = jnp.zeros((LINEAR_HEADS, DH, DH), jnp.float32)
    final_state, outputs = lax.scan(advance, start_state, (query_parts, key_parts, value_parts, decay_parts, doc_parts, block_starts))
    return outputs.reshape(TOKEN_COUNT, LINEAR_HEADS * DH)

def softmax_layer(query_soft, key_soft, value_soft, doc_start):
    group_size = SOFT_HEADS // KV_HEADS
    blocks = TOKEN_COUNT // TOK_DEV
    keys_float = key_soft.astype(jnp.float32).reshape(TOKEN_COUNT, KV_HEADS, DH)
    values_float = value_soft.astype(jnp.float32).reshape(TOKEN_COUNT, KV_HEADS, DH)
    token_positions = jnp.arange(TOKEN_COUNT, dtype=jnp.int32)
    query_parts = query_soft.reshape(blocks, TOK_DEV, KV_HEADS, group_size, DH)
    doc_parts = doc_start.reshape(blocks, TOK_DEV)
    block_starts = jnp.arange(blocks, dtype=jnp.int32) * TOK_DEV

    def one_block(slices):
        query_block, doc_block, first_place = slices
        query_places = first_place + jnp.arange(TOK_DEV, dtype=jnp.int32)
        allowed = (token_positions[None, :] <= query_places[:, None]) & (doc_block[:, None] <= token_positions[None, :])
        allowed = allowed[:, None, None, :]
        scores = jnp.einsum('tkgd,skd->tkgs', query_block.astype(jnp.float32), keys_float, precision=HIGHEST) * DH ** (-0.5)
        masked = jnp.where(allowed, scores, -jnp.inf)
        row_max = lax.optimization_barrier(jnp.max(masked, axis=-1, keepdims=True))
        raw_weight = jnp.where(allowed, jnp.exp(masked - row_max), 0.0)
        norm_sum = lax.optimization_barrier(jnp.sum(raw_weight, axis=-1))
        rounded = lax.optimization_barrier(raw_weight.astype(jnp.bfloat16))
        mixed_out = jnp.einsum('tkgs,skd->tkgd', rounded.astype(jnp.float32), values_float, precision=HIGHEST)
        soft_rows = (mixed_out / norm_sum[..., None]).astype(jnp.bfloat16).reshape(TOK_DEV, SOFT_HEADS * DH)
        lse_rows = (row_max[..., 0] + jnp.log(norm_sum)).reshape(TOK_DEV, SOFT_HEADS)
        return (soft_rows, lse_rows)
    soft_parts, lse_parts = lax.map(one_block, (query_parts, doc_parts, block_starts))
    soft_out = soft_parts.reshape(TOKEN_COUNT, SOFT_HEADS * DH)
    soft_lse = jnp.transpose(lse_parts.reshape(TOKEN_COUNT, SOFT_HEADS))
    return (soft_out, soft_lse)

def reference(query_lin, key_lin, value_lin, log_decay, query_soft, key_soft, value_soft, doc_start):
    lin_out = lightning(query_lin, key_lin, value_lin, log_decay, doc_start)
    soft_out, soft_lse = softmax_layer(query_soft, key_soft, value_soft, doc_start)
    return (lin_out, soft_out, soft_lse)
```

```python
import functools

import jax
import jax.numpy as jnp
from jax import lax
from jax.experimental import pallas as pl
from jax.experimental.pallas import tpu as pltpu
from jax.sharding import PartitionSpec as P


DH = 128


HIGHEST = lax.Precision.HIGHEST
masked_score = -1e30


def prefix(array, axis, combine, identity):
    size, here = (lax.axis_size(axis), lax.axis_index(axis))
    everything = jax.tree.map(lambda part: lax.all_gather(part, axis), array)
    start = jax.tree.map(
        lambda part, zero: jnp.broadcast_to(jnp.asarray(zero, part.dtype), part.shape),
        array,
        identity,
    )

    def lap(k, before):
        reached = k < here
        new = combine(before, jax.tree.map(lambda part: part[k], everything))
        return jax.tree.map(lambda a, b: jnp.where(reached, a, b), new, before)

    return lax.fori_loop(0, size, lap, start)


def span_terms(query_heads, key_heads, value_heads, decay_rows, doc_rows, first_place):
    span_len = query_heads.shape[0]
    cumulative = jnp.cumsum(decay_rows, axis=1)
    totals = cumulative[:, -1]
    token_positions = first_place + jnp.arange(span_len, dtype=jnp.int32)
    allowed = (token_positions[None, :] <= token_positions[:, None]) & (
        doc_rows[:, None] <= token_positions[None, :]
    )
    decay_gap = jnp.where(allowed[None], cumulative[:, :, None] - cumulative[:, None, :], 0.0)
    decay_mat = jnp.where(allowed[None], jnp.exp(decay_gap), 0.0)
    scores = jnp.einsum("thd,shd->hts", query_heads, key_heads, preferred_element_type=jnp.float32)
    key_float = key_heads.astype(jnp.float32)
    value_float = value_heads.astype(jnp.float32)
    inner_part = jnp.einsum("hts,shd->thd", scores * decay_mat, value_float, precision=HIGHEST)
    keep_mask = (doc_rows == doc_rows[-1]).astype(jnp.float32)
    tail_weight = jnp.exp(totals[:, None] - cumulative) * keep_mask[None, :]
    weighted_keys = key_float * jnp.transpose(tail_weight)[:, :, None]
    fresh_state = jnp.einsum("shd,she->hde", weighted_keys, value_float, precision=HIGHEST)
    carry_on = (doc_rows[-1] < first_place).astype(jnp.float32)
    factor = jnp.exp(totals) * carry_on
    read_mask = (doc_rows < first_place).astype(jnp.float32)[:, None] * jnp.transpose(
        jnp.exp(cumulative)
    )
    return (inner_part, fresh_state, factor, read_mask)


def combine_states(earlier, later_part):
    return (earlier[0] * later_part[0], later_part[0][:, None, None] * earlier[1] + later_part[1])


def lightning_part(query_lin, key_lin, value_lin, log_decay, doc_start):
    span_len = query_lin.shape[0]
    head_count = log_decay.shape[0]
    first_place = lax.axis_index("seq") * span_len
    query_heads = query_lin.reshape(span_len, head_count, DH)
    key_heads = key_lin.reshape(span_len, head_count, DH)
    value_heads = value_lin.reshape(span_len, head_count, DH)
    inner_part, fresh_state, factor, read_mask = span_terms(
        query_heads, key_heads, value_heads, log_decay, doc_start, first_place
    )
    identity = (jnp.ones((head_count,), jnp.float32), jnp.zeros((head_count, DH, DH), jnp.float32))
    unused, carried = prefix((factor, fresh_state), "seq", combine_states, identity)
    outer_part = (
        jnp.einsum("thd,hde->the", query_heads.astype(jnp.float32), carried, precision=HIGHEST)
        * read_mask[:, :, None]
    )
    mixed_out = inner_part + outer_part
    normed = mixed_out * lax.rsqrt(jnp.mean(mixed_out * mixed_out, axis=-1, keepdims=True) + 1e-06)
    return normed.astype(jnp.bfloat16).reshape(span_len, head_count * DH)


def softmax_part(query_soft, key_soft, value_soft, doc_start):
    queries, keys_local, values_local = (
        lax.all_to_all(query_soft, "head", split_axis=1, concat_axis=0, tiled=True),
        lax.all_to_all(key_soft, "head", split_axis=1, concat_axis=0, tiled=True),
        lax.all_to_all(value_soft, "head", split_axis=1, concat_axis=0, tiled=True),
    )
    span_len = queries.shape[0]
    kv_count = keys_local.shape[1] // DH
    group_size = queries.shape[1] // keys_local.shape[1]
    first_place = lax.axis_index("seq") * span_len
    query_places = first_place + jnp.arange(span_len, dtype=jnp.int32)
    query_heads = queries.reshape(span_len, kv_count, group_size, DH)
    score_scale = DH ** (-0.5)
    start_state = (
        jnp.full((span_len, kv_count, group_size), masked_score, jnp.float32),
        jnp.zeros((span_len, kv_count, group_size), jnp.float32),
        jnp.zeros((span_len, kv_count, group_size, DH), jnp.float32),
    )
    key_piece = lax.all_gather(keys_local, "seq", axis=0, tiled=True)
    value_piece = lax.all_gather(values_local, "seq", axis=0, tiled=True)
    piece_rows = key_piece.shape[0]
    block_rows = max(
        (divisor for divisor in range(1, min(piece_rows, 1024) + 1) if piece_rows % divisor == 0)
    )
    block_count = piece_rows // block_rows
    key_parts = key_piece.reshape(block_count, block_rows, kv_count, DH)
    value_parts = value_piece.reshape(block_count, block_rows, kv_count, DH)
    begin_rows = jnp.int32(0) + block_rows * jnp.arange(block_count, dtype=jnp.int32)

    def absorb_block(running, slices):
        key_block, value_block, begin_row = slices
        running_max, norm_sum, accum_out = running
        token_positions = begin_row + jnp.arange(block_rows, dtype=jnp.int32)
        allowed = (token_positions[None, :] <= query_places[:, None]) & (
            doc_start[:, None] <= token_positions[None, :]
        )
        allowed = allowed[:, None, None, :]
        scores = (
            jnp.einsum("tkgd,skd->tkgs", query_heads, key_block, preferred_element_type=jnp.float32)
            * score_scale
        )
        new_max = jnp.maximum(
            running_max, jnp.max(jnp.where(allowed, scores, masked_score), axis=-1)
        )
        raw_weight = jnp.where(allowed, jnp.exp(scores - new_max[..., None]), 0.0)
        shrink = jnp.exp(running_max - new_max)
        norm_sum = norm_sum * shrink + jnp.sum(raw_weight, axis=-1)
        accum_out = accum_out * shrink[..., None] + jnp.einsum(
            "tkgs,skd->tkgd",
            raw_weight.astype(jnp.bfloat16),
            value_block,
            preferred_element_type=jnp.float32,
        )
        running = (new_max, norm_sum, accum_out)
        return (running, None)

    final_state, unused = lax.scan(absorb_block, start_state, (key_parts, value_parts, begin_rows))
    running_max, norm_sum, accum_out = final_state
    soft_out = (
        (accum_out / norm_sum[..., None])
        .astype(jnp.bfloat16)
        .reshape(span_len, kv_count * group_size * DH)
    )
    soft_lse = jnp.transpose(
        (running_max + jnp.log(norm_sum)).reshape(span_len, kv_count * group_size)
    )
    return (soft_out, soft_lse)


MESH = pl.DeviceIdType.MESH
NT = (((1,), (1,)), ((), ()))


def fused_kernel(
    n, m, q_in, k_in, v_in, ld_in, qs_in, ks_in, vs_in, doc_in,
    lin_out, soft_out, lse_out,
    stage, lin_all, aux, aux_all, ld_v, doc_v, qs, kv, lin_v, soft_v, lse_v, bias,
    loc_sem, lin_s, lin_r, aux_s, aux_r, kv1_s, kv1_r, qs_s, qs_r, kv2_s, kv2_r, out_s, out_r,
):
    span, heads = doc_in.shape[1], ld_in.shape[0]
    rows = qs_in.shape[0]
    tokens = n * span
    me, hd = lax.axis_index("seq"), lax.axis_index("head")

    barrier = pltpu.get_barrier_semaphore()
    seq_peers = [lax.rem(me + j, n) for j in range(1, n)]
    head_peers = [lax.rem(hd + j, m) for j in range(1, m)]
    for peer in seq_peers:
        pl.semaphore_signal(barrier, inc=1, device_id={"seq": peer}, device_id_type=MESH)
    for peer in head_peers:
        pl.semaphore_signal(barrier, inc=1, device_id={"head": peer}, device_id_type=MESH)

    def cols(index, width=DH):
        return pl.ds(pl.multiple_of(index * width, width), width)

    def own_rows(index, count):
        return pl.ds(pl.multiple_of(index * count, count), count)

    loads = [
        pltpu.make_async_copy(ld_in, ld_v, loc_sem.at[0]),
        pltpu.make_async_copy(doc_in, doc_v, loc_sem.at[1]),
        pltpu.make_async_copy(q_in, stage.at[0], loc_sem.at[2]),
        pltpu.make_async_copy(k_in, stage.at[1], loc_sem.at[3]),
        pltpu.make_async_copy(v_in, stage.at[2], loc_sem.at[4]),
        pltpu.make_async_copy(
            ks_in.at[:, cols(hd)], kv.at[0, own_rows(me * m + hd, rows), :], loc_sem.at[5]
        ),
        pltpu.make_async_copy(
            vs_in.at[:, cols(hd)], kv.at[1, own_rows(me * m + hd, rows), :], loc_sem.at[6]
        ),
        pltpu.make_async_copy(
            qs_in.at[:, cols(hd, heads * DH)], qs.at[own_rows(hd, rows), :], loc_sem.at[7]
        ),
    ]
    for load in loads:
        load.start()
    aux[...] = jnp.zeros_like(aux)
    loads[0].wait()
    loads[1].wait()
    aux[0:heads, 0:span] = ld_v[...]
    aux[heads : heads + 1, 0:span] = doc_v[...].astype(jnp.float32)
    aux_all[me] = aux[...]
    for load in loads[2:5]:
        load.wait()
    own = pltpu.make_async_copy(
        stage.at[:, :, cols(me)], lin_all.at[:, own_rows(me, span), :], loc_sem.at[8]
    )
    own.start()
    pl.semaphore_wait(barrier, n + m - 2)

    def remote(src, dst, send, recv, device):
        return pltpu.make_async_remote_copy(
            src_ref=src, dst_ref=dst, send_sem=send, recv_sem=recv,
            device_id=device, device_id_type=MESH,
        )

    kv1, qsc = [], []
    for j, peer in enumerate(head_peers):
        dst_rows = own_rows(me * m + hd, rows)
        for side, src in enumerate((ks_in, vs_in)):
            kv1.append(
                remote(
                    src.at[:, cols(peer)], kv.at[side, dst_rows, :],
                    kv1_s.at[2 * j + side], kv1_r.at[2 * j + side], {"head": peer},
                )
            )
        qsc.append(
            remote(
                qs_in.at[:, cols(peer, heads * DH)], qs.at[own_rows(hd, rows), :],
                qs_s.at[j], qs_r.at[j], {"head": peer},
            )
        )
    auxc = [
        remote(aux, aux_all.at[me], aux_s.at[j], aux_r.at[j], {"seq": peer})
        for j, peer in enumerate(seq_peers)
    ]
    linc = [
        remote(
            stage.at[:, :, cols(peer)], lin_all.at[:, own_rows(me, span), :],
            lin_s.at[j], lin_r.at[j], {"seq": peer},
        )
        for j, peer in enumerate(seq_peers)
    ]
    mine = kv.at[:, own_rows(me, span), :]
    kv2 = [
        remote(mine, mine, kv2_s.at[j], kv2_r.at[j], {"seq": peer})
        for j, peer in enumerate(seq_peers)
    ]
    outc = [
        remote(
            lin_v.at[own_rows(peer, span), :], lin_out.at[:, cols(me)],
            out_s.at[j], out_r.at[j], {"seq": peer},
        )
        for j, peer in enumerate(seq_peers)
    ]
    for copy in kv1 + auxc + linc + qsc:
        copy.start()
    loads[5].wait()
    loads[6].wait()
    for copy in kv1:
        copy.wait_recv()
    for copy in kv2:
        copy.start()

    def iota(shape, dim):
        return lax.broadcasted_iota(jnp.int32, shape, dim)

    eye_s = iota((span, span), 0) == iota((span, span), 1)
    doc_col = jnp.sum(jnp.where(eye_s, doc_v[...].astype(jnp.float32), 0.0), axis=1, keepdims=True)
    place = me * span + iota((span, tokens), 0)
    key_at = iota((span, tokens), 1)
    open_s = (key_at <= place) & (key_at >= doc_col.astype(jnp.int32))
    half = jnp.where(open_s, 0.0, masked_score)
    bias[0:span, :] = half
    bias[span : 2 * span, :] = half

    for copy in auxc:
        copy.wait_recv()
    blk = 2 * span
    eye = iota((blk, blk), 0) == iota((blk, blk), 1)
    tri = iota((blk, blk), 0) >= iota((blk, blk), 1)
    sum_col, sum_row, doc_cols = [], [], []
    before = jnp.zeros((1, 1), jnp.float32)
    for i in range(tokens // blk):
        decay = jnp.concatenate(
            [aux_all[2 * i + b, pl.ds(me, 1), 0:span] for b in range(2)], axis=1
        )
        docs = jnp.concatenate(
            [aux_all[2 * i + b, heads : heads + 1, 0:span] for b in range(2)], axis=1
        )
        column = jnp.sum(jnp.where(tri, decay, 0.0), axis=1, keepdims=True) + before
        before = before + jnp.sum(decay, axis=1, keepdims=True)
        sum_col.append(column)
        sum_row.append(jnp.sum(jnp.where(eye, column, 0.0), axis=0, keepdims=True))
        doc_cols.append(jnp.sum(jnp.where(eye, docs, 0.0), axis=1, keepdims=True).astype(jnp.int32))

    own.wait()
    for copy in linc:
        copy.wait_recv()
    for i in range(tokens // blk):
        here = slice(i * blk, (i + 1) * blk)
        reach = (i + 1) * blk
        score = lax.dot_general(
            lin_all[0, here, :], lin_all[1, 0:reach, :], NT, preferred_element_type=jnp.float32
        )
        gap = sum_col[i] - jnp.concatenate(sum_row[: i + 1], axis=1)
        at = iota((blk, reach), 1)
        is_open = (at >= doc_cols[i]) & (at <= i * blk + iota((blk, reach), 0))
        mix = jnp.where(is_open, score * jnp.exp(gap), 0.0)
        out = jnp.dot(
            mix.astype(jnp.bfloat16), lin_all[2, 0:reach, :], preferred_element_type=jnp.float32
        )
        normed = out * lax.rsqrt(jnp.mean(out * out, axis=1, keepdims=True) + 1e-06)
        lin_v[here, :] = normed.astype(jnp.bfloat16)
    for copy in outc:
        copy.start()
    own_out = pltpu.make_async_copy(
        lin_v.at[own_rows(me, span), :], lin_out.at[:, cols(me)], loc_sem.at[9]
    )
    own_out.start()

    loads[7].wait()
    for copy in qsc + kv2:
        copy.wait_recv()
    stores = []
    for i in range(heads // 2):
        queries = jnp.concatenate(
            [qs[:, g * DH : (g + 1) * DH] for g in (2 * i, 2 * i + 1)], axis=0
        )
        score = lax.dot_general(queries, kv[0], NT, preferred_element_type=jnp.float32)
        score = score * DH ** (-0.5) + bias[...]
        top = jnp.max(score, axis=1, keepdims=True)
        weight = jnp.exp(score - top)
        total = jnp.sum(weight, axis=1, keepdims=True)
        out = jnp.dot(weight.astype(jnp.bfloat16), kv[1], preferred_element_type=jnp.float32)
        out = (out / total).astype(jnp.bfloat16)
        lse = top + jnp.log(total)
        for b in range(2):
            g = 2 * i + b
            part = slice(b * span, (b + 1) * span)
            soft_v[:, g * DH : (g + 1) * DH] = out[part]
            lse_v[g : g + 1, :] = jnp.sum(
                jnp.where(eye_s, lse[part], 0.0), axis=0, keepdims=True
            )
        pair = slice(2 * i * DH, 2 * (i + 1) * DH)
        stores.append(
            pltpu.make_async_copy(soft_v.at[:, pair], soft_out.at[:, pair], loc_sem.at[10 + i])
        )
        stores[-1].start()
    stores.append(pltpu.make_async_copy(lse_v, lse_out, loc_sem.at[10 + heads // 2]))
    stores[-1].start()

    for copy in outc:
        copy.wait_recv()
    own_out.wait()
    for copy in stores:
        copy.wait()
    for copy in kv1 + auxc + linc + qsc + kv2 + outc:
        copy.wait_send()


def fused(n, m, query_lin, key_lin, value_lin, log_decay, query_soft, key_soft, value_soft, doc_start):
    span, heads = query_lin.shape[0], log_decay.shape[0]
    tokens, rows = n * span, query_soft.shape[0]
    bf16, f32 = jnp.bfloat16, jnp.float32
    any_spec = pl.BlockSpec(memory_space=pl.ANY)
    dma = pltpu.SemaphoreType.DMA
    return pl.pallas_call(
        functools.partial(fused_kernel, n, m),
        out_shape=(
            jax.ShapeDtypeStruct((span, heads * DH), bf16),
            jax.ShapeDtypeStruct((span, heads * DH), bf16),
            jax.ShapeDtypeStruct((heads, span), f32),
        ),
        in_specs=[any_spec] * 8,
        out_specs=(any_spec,) * 3,
        scratch_shapes=[
            pltpu.VMEM((3, span, heads * DH), bf16),
            pltpu.VMEM((3, tokens, DH), bf16),
            pltpu.VMEM((2 * heads, DH), f32),
            pltpu.VMEM((n, 2 * heads, DH), f32),
            pltpu.VMEM((heads, span), f32),
            pltpu.VMEM((1, span), jnp.int32),
            pltpu.VMEM((span, heads * DH), bf16),
            pltpu.VMEM((2, tokens, DH), bf16),
            pltpu.VMEM((tokens, DH), bf16),
            pltpu.VMEM((span, heads * DH), bf16),
            pltpu.VMEM((heads, span), f32),
            pltpu.VMEM((2 * span, tokens), f32),
            dma((11 + heads // 2,)),
        ]
        + [dma((n - 1,))] * 4
        + [dma((2 * (m - 1),))] * 2
        + [dma((m - 1,))] * 2
        + [dma((n - 1,))] * 4,
        compiler_params=pltpu.CompilerParams(
            collective_id=0, has_side_effects=True, vmem_limit_bytes=32 * 1024 * 1024
        ),
    )(
        query_lin, key_lin, value_lin, log_decay, query_soft, key_soft, value_soft,
        doc_start.reshape(1, span),
    )


def per_device(
    query_lin, key_lin, value_lin, log_decay, query_soft, key_soft, value_soft, doc_start
):
    n, m = lax.axis_size("seq"), lax.axis_size("head")
    span, heads = query_lin.shape[0], log_decay.shape[0]
    if heads == n and span == DH // 2 and key_soft.shape[1] == m * DH and n % 2 == 0:
        return fused(
            n, m, query_lin, key_lin, value_lin, log_decay,
            query_soft, key_soft, value_soft, doc_start,
        )
    lin_out = lightning_part(query_lin, key_lin, value_lin, log_decay, doc_start)
    soft_out, soft_lse = softmax_part(query_soft, key_soft, value_soft, doc_start)
    return (lin_out, soft_out, soft_lse)


def solution(mesh):
    return jax.shard_map(
        per_device,
        mesh=mesh,
        in_specs=(
            P("seq", "head"),
            P("seq", "head"),
            P("seq", "head"),
            P("head", "seq"),
            P(("seq", "head"), None),
            P(("seq", "head"), None),
            P(("seq", "head"), None),
            P("seq"),
        ),
        out_specs=(P("seq", "head"), P("seq", "head"), P("head", "seq")),
        check_vma=False,
    )
```

```python
import functools

import jax
import jax.numpy as jnp
from jax import lax
from jax.experimental import pallas as pl
from jax.experimental.pallas import tpu as pltpu
from jax.sharding import PartitionSpec as P


DH = 128


HIGHEST = lax.Precision.HIGHEST
masked_score = -1e30


def prefix(array, axis, combine, identity):
    size, here = (lax.axis_size(axis), lax.axis_index(axis))
    everything = jax.tree.map(lambda part: lax.all_gather(part, axis), array)
    start = jax.tree.map(
        lambda part, zero: jnp.broadcast_to(jnp.asarray(zero, part.dtype), part.shape),
        array,
        identity,
    )

    def lap(k, before):
        reached = k < here
        new = combine(before, jax.tree.map(lambda part: part[k], everything))
        return jax.tree.map(lambda a, b: jnp.where(reached, a, b), new, before)

    return lax.fori_loop(0, size, lap, start)


def span_terms(query_heads, key_heads, value_heads, decay_rows, doc_rows, first_place):
    span_len = query_heads.shape[0]
    cumulative = jnp.cumsum(decay_rows, axis=1)
    totals = cumulative[:, -1]
    token_positions = first_place + jnp.arange(span_len, dtype=jnp.int32)
    allowed = (token_positions[None, :] <= token_positions[:, None]) & (
        doc_rows[:, None] <= token_positions[None, :]
    )
    decay_gap = jnp.where(allowed[None], cumulative[:, :, None] - cumulative[:, None, :], 0.0)
    decay_mat = jnp.where(allowed[None], jnp.exp(decay_gap), 0.0)
    scores = jnp.einsum("thd,shd->hts", query_heads, key_heads, preferred_element_type=jnp.float32)
    key_float = key_heads.astype(jnp.float32)
    value_float = value_heads.astype(jnp.float32)
    inner_part = jnp.einsum("hts,shd->thd", scores * decay_mat, value_float, precision=HIGHEST)
    keep_mask = (doc_rows == doc_rows[-1]).astype(jnp.float32)
    tail_weight = jnp.exp(totals[:, None] - cumulative) * keep_mask[None, :]
    weighted_keys = key_float * jnp.transpose(tail_weight)[:, :, None]
    fresh_state = jnp.einsum("shd,she->hde", weighted_keys, value_float, precision=HIGHEST)
    carry_on = (doc_rows[-1] < first_place).astype(jnp.float32)
    factor = jnp.exp(totals) * carry_on
    read_mask = (doc_rows < first_place).astype(jnp.float32)[:, None] * jnp.transpose(
        jnp.exp(cumulative)
    )
    return (inner_part, fresh_state, factor, read_mask)


def combine_states(earlier, later_part):
    return (earlier[0] * later_part[0], later_part[0][:, None, None] * earlier[1] + later_part[1])


def lightning_part(query_lin, key_lin, value_lin, log_decay, doc_start):
    span_len = query_lin.shape[0]
    head_count = log_decay.shape[0]
    first_place = lax.axis_index("seq") * span_len
    query_heads = query_lin.reshape(span_len, head_count, DH)
    key_heads = key_lin.reshape(span_len, head_count, DH)
    value_heads = value_lin.reshape(span_len, head_count, DH)
    inner_part, fresh_state, factor, read_mask = span_terms(
        query_heads, key_heads, value_heads, log_decay, doc_start, first_place
    )
    identity = (jnp.ones((head_count,), jnp.float32), jnp.zeros((head_count, DH, DH), jnp.float32))
    unused, carried = prefix((factor, fresh_state), "seq", combine_states, identity)
    outer_part = (
        jnp.einsum("thd,hde->the", query_heads.astype(jnp.float32), carried, precision=HIGHEST)
        * read_mask[:, :, None]
    )
    mixed_out = inner_part + outer_part
    normed = mixed_out * lax.rsqrt(jnp.mean(mixed_out * mixed_out, axis=-1, keepdims=True) + 1e-06)
    return normed.astype(jnp.bfloat16).reshape(span_len, head_count * DH)


def softmax_part(query_soft, key_soft, value_soft, doc_start):
    queries, keys_local, values_local = (
        lax.all_to_all(query_soft, "head", split_axis=1, concat_axis=0, tiled=True),
        lax.all_to_all(key_soft, "head", split_axis=1, concat_axis=0, tiled=True),
        lax.all_to_all(value_soft, "head", split_axis=1, concat_axis=0, tiled=True),
    )
    span_len = queries.shape[0]
    kv_count = keys_local.shape[1] // DH
    group_size = queries.shape[1] // keys_local.shape[1]
    first_place = lax.axis_index("seq") * span_len
    query_places = first_place + jnp.arange(span_len, dtype=jnp.int32)
    query_heads = queries.reshape(span_len, kv_count, group_size, DH)
    score_scale = DH ** (-0.5)
    start_state = (
        jnp.full((span_len, kv_count, group_size), masked_score, jnp.float32),
        jnp.zeros((span_len, kv_count, group_size), jnp.float32),
        jnp.zeros((span_len, kv_count, group_size, DH), jnp.float32),
    )
    key_piece = lax.all_gather(keys_local, "seq", axis=0, tiled=True)
    value_piece = lax.all_gather(values_local, "seq", axis=0, tiled=True)
    piece_rows = key_piece.shape[0]
    block_rows = max(
        (divisor for divisor in range(1, min(piece_rows, 1024) + 1) if piece_rows % divisor == 0)
    )
    block_count = piece_rows // block_rows
    key_parts = key_piece.reshape(block_count, block_rows, kv_count, DH)
    value_parts = value_piece.reshape(block_count, block_rows, kv_count, DH)
    begin_rows = jnp.int32(0) + block_rows * jnp.arange(block_count, dtype=jnp.int32)

    def absorb_block(running, slices):
        key_block, value_block, begin_row = slices
        running_max, norm_sum, accum_out = running
        token_positions = begin_row + jnp.arange(block_rows, dtype=jnp.int32)
        allowed = (token_positions[None, :] <= query_places[:, None]) & (
            doc_start[:, None] <= token_positions[None, :]
        )
        allowed = allowed[:, None, None, :]
        scores = (
            jnp.einsum("tkgd,skd->tkgs", query_heads, key_block, preferred_element_type=jnp.float32)
            * score_scale
        )
        new_max = jnp.maximum(
            running_max, jnp.max(jnp.where(allowed, scores, masked_score), axis=-1)
        )
        raw_weight = jnp.where(allowed, jnp.exp(scores - new_max[..., None]), 0.0)
        shrink = jnp.exp(running_max - new_max)
        norm_sum = norm_sum * shrink + jnp.sum(raw_weight, axis=-1)
        accum_out = accum_out * shrink[..., None] + jnp.einsum(
            "tkgs,skd->tkgd",
            raw_weight.astype(jnp.bfloat16),
            value_block,
            preferred_element_type=jnp.float32,
        )
        running = (new_max, norm_sum, accum_out)
        return (running, None)

    final_state, unused = lax.scan(absorb_block, start_state, (key_parts, value_parts, begin_rows))
    running_max, norm_sum, accum_out = final_state
    soft_out = (
        (accum_out / norm_sum[..., None])
        .astype(jnp.bfloat16)
        .reshape(span_len, kv_count * group_size * DH)
    )
    soft_lse = jnp.transpose(
        (running_max + jnp.log(norm_sum)).reshape(span_len, kv_count * group_size)
    )
    return (soft_out, soft_lse)


MESH = pl.DeviceIdType.MESH
NT = (((1,), (1,)), ((), ()))


def fused_kernel(
    n, m, q_in, k_in, v_in, ld_in, qs_in, ks_in, vs_in, doc_in,
    lin_out, soft_out, lse_out,
    stage, lin_all, aux, aux_all, ld_v, doc_v, qs, kv, lin_v, soft_v, lse_v, bias,
    loc_sem, lin_s, lin_r, aux_s, aux_r, kv1_s, kv1_r, qs_s, qs_r, kv2_s, kv2_r, out_s, out_r,
):
    span, heads = doc_in.shape[1], ld_in.shape[0]
    rows = qs_in.shape[0]
    tokens = n * span
    me, hd = lax.axis_index("seq"), lax.axis_index("head")

    barrier = pltpu.get_barrier_semaphore()
    seq_peers = [lax.rem(me + j, n) for j in range(1, n)]
    head_peers = [lax.rem(hd + j, m) for j in range(1, m)]
    for peer in seq_peers:
        pl.semaphore_signal(barrier, inc=1, device_id={"seq": peer}, device_id_type=MESH)
    for peer in head_peers:
        pl.semaphore_signal(barrier, inc=1, device_id={"head": peer}, device_id_type=MESH)

    def cols(index, width=DH):
        return pl.ds(pl.multiple_of(index * width, width), width)

    def own_rows(index, count):
        return pl.ds(pl.multiple_of(index * count, count), count)

    loads = [
        pltpu.make_async_copy(ld_in, ld_v, loc_sem.at[0]),
        pltpu.make_async_copy(doc_in, doc_v, loc_sem.at[1]),
        pltpu.make_async_copy(q_in, stage.at[0], loc_sem.at[2]),
        pltpu.make_async_copy(k_in, stage.at[1], loc_sem.at[3]),
        pltpu.make_async_copy(v_in, stage.at[2], loc_sem.at[4]),
        pltpu.make_async_copy(
            ks_in.at[:, cols(hd)], kv.at[0, own_rows(me * m + hd, rows), :], loc_sem.at[5]
        ),
        pltpu.make_async_copy(
            vs_in.at[:, cols(hd)], kv.at[1, own_rows(me * m + hd, rows), :], loc_sem.at[6]
        ),
        pltpu.make_async_copy(
            qs_in.at[:, cols(hd, heads * DH)], qs.at[own_rows(hd, rows), :], loc_sem.at[7]
        ),
    ]
    for load in loads:
        load.start()
    aux[...] = jnp.zeros_like(aux)
    loads[0].wait()
    loads[1].wait()
    aux[0:heads, 0:span] = ld_v[...]
    aux[heads : heads + 1, 0:span] = doc_v[...].astype(jnp.float32)
    aux_all[me] = aux[...]
    for load in loads[2:5]:
        load.wait()
    own = pltpu.make_async_copy(
        stage.at[:, :, cols(me)], lin_all.at[:, own_rows(me, span), :], loc_sem.at[8]
    )
    own.start()
    pl.semaphore_wait(barrier, n + m - 2)

    def remote(src, dst, send, recv, device):
        return pltpu.make_async_remote_copy(
            src_ref=src, dst_ref=dst, send_sem=send, recv_sem=recv,
            device_id=device, device_id_type=MESH,
        )

    kv1, qsc = [], []
    for j, peer in enumerate(head_peers):
        dst_rows = own_rows(me * m + hd, rows)
        for side, src in enumerate((ks_in, vs_in)):
            kv1.append(
                remote(
                    src.at[:, cols(peer)], kv.at[side, dst_rows, :],
                    kv1_s.at[2 * j + side], kv1_r.at[2 * j + side], {"head": peer},
                )
            )
        qsc.append(
            remote(
                qs_in.at[:, cols(peer, heads * DH)], qs.at[own_rows(hd, rows), :],
                qs_s.at[j], qs_r.at[j], {"head": peer},
            )
        )
    auxc = [
        remote(aux, aux_all.at[me], aux_s.at[j], aux_r.at[j], {"seq": peer})
        for j, peer in enumerate(seq_peers)
    ]
    linc = [
        remote(
            stage.at[:, :, cols(peer)], lin_all.at[:, own_rows(me, span), :],
            lin_s.at[j], lin_r.at[j], {"seq": peer},
        )
        for j, peer in enumerate(seq_peers)
    ]
    mine = kv.at[:, own_rows(me, span), :]
    kv2 = [
        remote(mine, mine, kv2_s.at[j], kv2_r.at[j], {"seq": peer})
        for j, peer in enumerate(seq_peers)
    ]
    outc = [
        remote(
            lin_v.at[own_rows(peer, span), :], lin_out.at[:, cols(me)],
            out_s.at[j], out_r.at[j], {"seq": peer},
        )
        for j, peer in enumerate(seq_peers)
    ]
    for copy in kv1 + auxc + linc + qsc:
        copy.start()
    loads[5].wait()
    loads[6].wait()
    for copy in kv1:
        copy.wait_recv()
    for copy in kv2:
        copy.start()

    def iota(shape, dim):
        return lax.broadcasted_iota(jnp.int32, shape, dim)

    eye_s = iota((span, span), 0) == iota((span, span), 1)
    doc_col = jnp.sum(jnp.where(eye_s, doc_v[...].astype(jnp.float32), 0.0), axis=1, keepdims=True)
    place = me * span + iota((span, tokens), 0)
    key_at = iota((span, tokens), 1)
    open_s = (key_at <= place) & (key_at >= doc_col.astype(jnp.int32))
    half = jnp.where(open_s, 0.0, masked_score)
    bias[0:span, :] = half
    bias[span : 2 * span, :] = half

    for copy in auxc:
        copy.wait_recv()
    blk = 2 * span
    eye = iota((blk, blk), 0) == iota((blk, blk), 1)
    tri = iota((blk, blk), 0) >= iota((blk, blk), 1)
    sum_col, sum_row, doc_cols = [], [], []
    before = jnp.zeros((1, 1), jnp.float32)
    for i in range(tokens // blk):
        decay = jnp.concatenate(
            [aux_all[2 * i + b, pl.ds(me, 1), 0:span] for b in range(2)], axis=1
        )
        docs = jnp.concatenate(
            [aux_all[2 * i + b, heads : heads + 1, 0:span] for b in range(2)], axis=1
        )
        column = jnp.sum(jnp.where(tri, decay, 0.0), axis=1, keepdims=True) + before
        before = before + jnp.sum(decay, axis=1, keepdims=True)
        sum_col.append(column)
        sum_row.append(jnp.sum(jnp.where(eye, column, 0.0), axis=0, keepdims=True))
        doc_cols.append(jnp.sum(jnp.where(eye, docs, 0.0), axis=1, keepdims=True).astype(jnp.int32))

    own.wait()
    for copy in linc:
        copy.wait_recv()
    for i in range(tokens // blk):
        here = slice(i * blk, (i + 1) * blk)
        reach = (i + 1) * blk
        score = lax.dot_general(
            lin_all[0, here, :], lin_all[1, 0:reach, :], NT, preferred_element_type=jnp.float32
        )
        gap = sum_col[i] - jnp.concatenate(sum_row[: i + 1], axis=1)
        at = iota((blk, reach), 1)
        is_open = (at >= doc_cols[i]) & (at <= i * blk + iota((blk, reach), 0))
        mix = jnp.where(is_open, score * jnp.exp(gap), 0.0)
        high = mix.astype(jnp.bfloat16)
        low = (mix - high.astype(jnp.float32)).astype(jnp.bfloat16)
        values = lin_all[2, 0:reach, :]
        out = jnp.dot(high, values, preferred_element_type=jnp.float32) + jnp.dot(
            low, values, preferred_element_type=jnp.float32
        )
        normed = out * lax.rsqrt(jnp.mean(out * out, axis=1, keepdims=True) + 1e-06)
        lin_v[here, :] = normed.astype(jnp.bfloat16)
    for copy in outc:
        copy.start()
    own_out = pltpu.make_async_copy(
        lin_v.at[own_rows(me, span), :], lin_out.at[:, cols(me)], loc_sem.at[9]
    )
    own_out.start()

    loads[7].wait()
    for copy in qsc + kv2:
        copy.wait_recv()
    stores = []
    for i in range(heads // 2):
        queries = jnp.concatenate(
            [qs[:, g * DH : (g + 1) * DH] for g in (2 * i, 2 * i + 1)], axis=0
        )
        score = lax.dot_general(queries, kv[0], NT, preferred_element_type=jnp.float32)
        score = score * DH ** (-0.5) + bias[...]
        top = jnp.max(score, axis=1, keepdims=True)
        weight = jnp.exp(score - top)
        total = jnp.sum(weight, axis=1, keepdims=True)
        out = jnp.dot(weight.astype(jnp.bfloat16), kv[1], preferred_element_type=jnp.float32)
        out = (out / total).astype(jnp.bfloat16)
        lse = top + jnp.log(total)
        for b in range(2):
            g = 2 * i + b
            part = slice(b * span, (b + 1) * span)
            soft_v[:, g * DH : (g + 1) * DH] = out[part]
            lse_v[g : g + 1, :] = jnp.sum(
                jnp.where(eye_s, lse[part], 0.0), axis=0, keepdims=True
            )
        pair = slice(2 * i * DH, 2 * (i + 1) * DH)
        stores.append(
            pltpu.make_async_copy(soft_v.at[:, pair], soft_out.at[:, pair], loc_sem.at[10 + i])
        )
        stores[-1].start()
    stores.append(pltpu.make_async_copy(lse_v, lse_out, loc_sem.at[10 + heads // 2]))
    stores[-1].start()

    for copy in outc:
        copy.wait_recv()
    own_out.wait()
    for copy in stores:
        copy.wait()
    for copy in kv1 + auxc + linc + qsc + kv2 + outc:
        copy.wait_send()


def fused(n, m, query_lin, key_lin, value_lin, log_decay, query_soft, key_soft, value_soft, doc_start):
    span, heads = query_lin.shape[0], log_decay.shape[0]
    tokens, rows = n * span, query_soft.shape[0]
    bf16, f32 = jnp.bfloat16, jnp.float32
    any_spec = pl.BlockSpec(memory_space=pl.ANY)
    hbm_spec = pl.BlockSpec(memory_space=pltpu.HBM)
    dma = pltpu.SemaphoreType.DMA
    results = pl.pallas_call(
        functools.partial(fused_kernel, n, m),
        out_shape=(
            jax.ShapeDtypeStruct((span, heads * DH), bf16),
            jax.ShapeDtypeStruct((span, heads * DH), bf16),
            jax.ShapeDtypeStruct((heads, span), f32),
        ),
        in_specs=[any_spec] * 8,
        out_specs=(any_spec,) * 3,
        scratch_shapes=[
            pltpu.VMEM((3, span, heads * DH), bf16),
            pltpu.VMEM((3, tokens, DH), bf16),
            pltpu.VMEM((2 * heads, DH), f32),
            pltpu.VMEM((n, 2 * heads, DH), f32),
            pltpu.VMEM((heads, span), f32),
            pltpu.VMEM((1, span), jnp.int32),
            pltpu.VMEM((span, heads * DH), bf16),
            pltpu.VMEM((2, tokens, DH), bf16),
            pltpu.VMEM((tokens, DH), bf16),
            pltpu.VMEM((span, heads * DH), bf16),
            pltpu.VMEM((heads, span), f32),
            pltpu.VMEM((2 * span, tokens), f32),
            dma((11 + heads // 2,)),
        ]
        + [dma((n - 1,))] * 4
        + [dma((2 * (m - 1),))] * 2
        + [dma((m - 1,))] * 2
        + [dma((n - 1,))] * 4,
        compiler_params=pltpu.CompilerParams(
            collective_id=0, has_side_effects=True, vmem_limit_bytes=32 * 1024 * 1024
        ),
    )(*(pltpu.with_memory_space_constraint(x, pltpu.HBM) for x in (
        query_lin, key_lin, value_lin, log_decay, query_soft, key_soft, value_soft,
        doc_start.reshape(1, span),
    )))
    return pl.pallas_call(
        store_kernel,
        out_shape=tuple(jax.ShapeDtypeStruct(part.shape, part.dtype) for part in results),
        in_specs=[any_spec] * 3,
        out_specs=(hbm_spec,) * 3,
        scratch_shapes=[dma((3,))],
    )(*(pltpu.with_memory_space_constraint(part, pltpu.VMEM) for part in results))


def store_kernel(a, b, c, a_out, b_out, c_out, sem):
    copies = [
        pltpu.make_async_copy(src, dst, sem.at[i])
        for i, (src, dst) in enumerate(((a, a_out), (b, b_out), (c, c_out)))
    ]
    for copy in copies:
        copy.start()
    for copy in copies:
        copy.wait()


def per_device(
    query_lin, key_lin, value_lin, log_decay, query_soft, key_soft, value_soft, doc_start
):
    n, m = lax.axis_size("seq"), lax.axis_size("head")
    span, heads = query_lin.shape[0], log_decay.shape[0]
    if heads == n and span == DH // 2 and key_soft.shape[1] == m * DH and n % 2 == 0:
        return fused(
            n, m, query_lin, key_lin, value_lin, log_decay,
            query_soft, key_soft, value_soft, doc_start,
        )
    lin_out = lightning_part(query_lin, key_lin, value_lin, log_decay, doc_start)
    soft_out, soft_lse = softmax_part(query_soft, key_soft, value_soft, doc_start)
    return (lin_out, soft_out, soft_lse)


def solution(mesh):
    return jax.shard_map(
        per_device,
        mesh=mesh,
        in_specs=(
            P("seq", "head"),
            P("seq", "head"),
            P("seq", "head"),
            P("head", "seq"),
            P(("seq", "head"), None),
            P(("seq", "head"), None),
            P(("seq", "head"), None),
            P("seq"),
        ),
        out_specs=(P("seq", "head"), P("seq", "head"), P("head", "seq")),
        check_vma=False,
    )
```

```python
import functools

import jax
import jax.numpy as jnp
from jax import lax
from jax.experimental import pallas as pl
from jax.experimental.pallas import tpu as pltpu
from jax.sharding import PartitionSpec as P


DH = 128


HIGHEST = lax.Precision.HIGHEST
masked_score = -1e30


def prefix(array, axis, combine, identity):
    size, here = (lax.axis_size(axis), lax.axis_index(axis))
    everything = jax.tree.map(lambda part: lax.all_gather(part, axis), array)
    start = jax.tree.map(
        lambda part, zero: jnp.broadcast_to(jnp.asarray(zero, part.dtype), part.shape),
        array,
        identity,
    )

    def lap(k, before):
        reached = k < here
        new = combine(before, jax.tree.map(lambda part: part[k], everything))
        return jax.tree.map(lambda a, b: jnp.where(reached, a, b), new, before)

    return lax.fori_loop(0, size, lap, start)


def span_terms(query_heads, key_heads, value_heads, decay_rows, doc_rows, first_place):
    span_len = query_heads.shape[0]
    cumulative = jnp.cumsum(decay_rows, axis=1)
    totals = cumulative[:, -1]
    token_positions = first_place + jnp.arange(span_len, dtype=jnp.int32)
    allowed = (token_positions[None, :] <= token_positions[:, None]) & (
        doc_rows[:, None] <= token_positions[None, :]
    )
    decay_gap = jnp.where(allowed[None], cumulative[:, :, None] - cumulative[:, None, :], 0.0)
    decay_mat = jnp.where(allowed[None], jnp.exp(decay_gap), 0.0)
    scores = jnp.einsum("thd,shd->hts", query_heads, key_heads, preferred_element_type=jnp.float32)
    key_float = key_heads.astype(jnp.float32)
    value_float = value_heads.astype(jnp.float32)
    inner_part = jnp.einsum("hts,shd->thd", scores * decay_mat, value_float, precision=HIGHEST)
    keep_mask = (doc_rows == doc_rows[-1]).astype(jnp.float32)
    tail_weight = jnp.exp(totals[:, None] - cumulative) * keep_mask[None, :]
    weighted_keys = key_float * jnp.transpose(tail_weight)[:, :, None]
    fresh_state = jnp.einsum("shd,she->hde", weighted_keys, value_float, precision=HIGHEST)
    carry_on = (doc_rows[-1] < first_place).astype(jnp.float32)
    factor = jnp.exp(totals) * carry_on
    read_mask = (doc_rows < first_place).astype(jnp.float32)[:, None] * jnp.transpose(
        jnp.exp(cumulative)
    )
    return (inner_part, fresh_state, factor, read_mask)


def combine_states(earlier, later_part):
    return (earlier[0] * later_part[0], later_part[0][:, None, None] * earlier[1] + later_part[1])


def lightning_part(query_lin, key_lin, value_lin, log_decay, doc_start):
    span_len = query_lin.shape[0]
    head_count = log_decay.shape[0]
    first_place = lax.axis_index("seq") * span_len
    query_heads = query_lin.reshape(span_len, head_count, DH)
    key_heads = key_lin.reshape(span_len, head_count, DH)
    value_heads = value_lin.reshape(span_len, head_count, DH)
    inner_part, fresh_state, factor, read_mask = span_terms(
        query_heads, key_heads, value_heads, log_decay, doc_start, first_place
    )
    identity = (jnp.ones((head_count,), jnp.float32), jnp.zeros((head_count, DH, DH), jnp.float32))
    unused, carried = prefix((factor, fresh_state), "seq", combine_states, identity)
    outer_part = (
        jnp.einsum("thd,hde->the", query_heads.astype(jnp.float32), carried, precision=HIGHEST)
        * read_mask[:, :, None]
    )
    mixed_out = inner_part + outer_part
    normed = mixed_out * lax.rsqrt(jnp.mean(mixed_out * mixed_out, axis=-1, keepdims=True) + 1e-06)
    return normed.astype(jnp.bfloat16).reshape(span_len, head_count * DH)


def softmax_part(query_soft, key_soft, value_soft, doc_start):
    queries, keys_local, values_local = (
        lax.all_to_all(query_soft, "head", split_axis=1, concat_axis=0, tiled=True),
        lax.all_to_all(key_soft, "head", split_axis=1, concat_axis=0, tiled=True),
        lax.all_to_all(value_soft, "head", split_axis=1, concat_axis=0, tiled=True),
    )
    span_len = queries.shape[0]
    kv_count = keys_local.shape[1] // DH
    group_size = queries.shape[1] // keys_local.shape[1]
    first_place = lax.axis_index("seq") * span_len
    query_places = first_place + jnp.arange(span_len, dtype=jnp.int32)
    query_heads = queries.reshape(span_len, kv_count, group_size, DH)
    score_scale = DH ** (-0.5)
    start_state = (
        jnp.full((span_len, kv_count, group_size), masked_score, jnp.float32),
        jnp.zeros((span_len, kv_count, group_size), jnp.float32),
        jnp.zeros((span_len, kv_count, group_size, DH), jnp.float32),
    )
    key_piece = lax.all_gather(keys_local, "seq", axis=0, tiled=True)
    value_piece = lax.all_gather(values_local, "seq", axis=0, tiled=True)
    piece_rows = key_piece.shape[0]
    block_rows = max(
        (divisor for divisor in range(1, min(piece_rows, 1024) + 1) if piece_rows % divisor == 0)
    )
    block_count = piece_rows // block_rows
    key_parts = key_piece.reshape(block_count, block_rows, kv_count, DH)
    value_parts = value_piece.reshape(block_count, block_rows, kv_count, DH)
    begin_rows = jnp.int32(0) + block_rows * jnp.arange(block_count, dtype=jnp.int32)

    def absorb_block(running, slices):
        key_block, value_block, begin_row = slices
        running_max, norm_sum, accum_out = running
        token_positions = begin_row + jnp.arange(block_rows, dtype=jnp.int32)
        allowed = (token_positions[None, :] <= query_places[:, None]) & (
            doc_start[:, None] <= token_positions[None, :]
        )
        allowed = allowed[:, None, None, :]
        scores = (
            jnp.einsum("tkgd,skd->tkgs", query_heads, key_block, preferred_element_type=jnp.float32)
            * score_scale
        )
        new_max = jnp.maximum(
            running_max, jnp.max(jnp.where(allowed, scores, masked_score), axis=-1)
        )
        raw_weight = jnp.where(allowed, jnp.exp(scores - new_max[..., None]), 0.0)
        shrink = jnp.exp(running_max - new_max)
        norm_sum = norm_sum * shrink + jnp.sum(raw_weight, axis=-1)
        accum_out = accum_out * shrink[..., None] + jnp.einsum(
            "tkgs,skd->tkgd",
            raw_weight.astype(jnp.bfloat16),
            value_block,
            preferred_element_type=jnp.float32,
        )
        running = (new_max, norm_sum, accum_out)
        return (running, None)

    final_state, unused = lax.scan(absorb_block, start_state, (key_parts, value_parts, begin_rows))
    running_max, norm_sum, accum_out = final_state
    soft_out = (
        (accum_out / norm_sum[..., None])
        .astype(jnp.bfloat16)
        .reshape(span_len, kv_count * group_size * DH)
    )
    soft_lse = jnp.transpose(
        (running_max + jnp.log(norm_sum)).reshape(span_len, kv_count * group_size)
    )
    return (soft_out, soft_lse)


MESH = pl.DeviceIdType.MESH
NT = (((1,), (1,)), ((), ()))


def fused_kernel(
    n, m, q_in, k_in, v_in, ld_in, qs_in, ks_in, vs_in, doc_in,
    lin_out, soft_out, lse_out,
    stage, lin_all, aux, aux_all, ld_v, doc_v, qs, kvs, kv, lin_v, soft_v, lse_v, bias,
    loc_sem, lin_s, lin_r, aux_s, aux_r, kv1_s, kv1_r, qs_s, qs_r, kv2_s, kv2_r, out_s, out_r,
):
    span, heads = doc_in.shape[1], ld_in.shape[0]
    rows = qs_in.shape[0]
    tokens = n * span
    me, hd = lax.axis_index("seq"), lax.axis_index("head")

    kv[...] = jnp.zeros_like(kv)
    barrier = pltpu.get_barrier_semaphore()
    pair, core = me // 2, lax.rem(me, 2)
    far = [n // 2 - 1 - pair, pair + 1 - 2 * lax.rem(pair, 2)]
    far += [lax.rem(pair + j, n // 2) for j in range(2, n // 2, 2)]
    seq_peers = [2 * other + c for other in far for c in (core, 1 - core)] + [me + 1 - 2 * core]
    head_peers = [lax.rem(hd + j, m) for j in range(1, m)]
    for peer in head_peers:
        pl.semaphore_signal(barrier, inc=1, device_id={"head": peer}, device_id_type=MESH)
    for peer in seq_peers:
        pl.semaphore_signal(barrier, inc=1, device_id={"seq": peer}, device_id_type=MESH)

    def cols(index, width=DH):
        return pl.ds(pl.multiple_of(index * width, width), width)

    def own_rows(index, count):
        return pl.ds(pl.multiple_of(index * count, count), count)

    loads = [
        pltpu.make_async_copy(ld_in, ld_v, loc_sem.at[0]),
        pltpu.make_async_copy(doc_in, doc_v, loc_sem.at[1]),
        pltpu.make_async_copy(q_in, stage.at[0], loc_sem.at[2]),
        pltpu.make_async_copy(k_in, stage.at[1], loc_sem.at[3]),
        pltpu.make_async_copy(v_in, stage.at[2], loc_sem.at[4]),
        pltpu.make_async_copy(ks_in, kvs.at[0], loc_sem.at[5]),
        pltpu.make_async_copy(vs_in, kvs.at[1], loc_sem.at[6]),
        pltpu.make_async_copy(
            qs_in.at[:, cols(hd, heads * DH)], qs.at[own_rows(hd, rows), :], loc_sem.at[7]
        ),
    ]
    for load in loads:
        load.start()
    aux[...] = jnp.zeros_like(aux)
    loads[0].wait()
    loads[1].wait()
    aux[0:heads, 0:span] = ld_v[...]
    aux[heads : heads + 1, 0:span] = doc_v[...].astype(jnp.float32)
    aux_all[me] = aux[...]
    for load in loads[2:7]:
        load.wait()
    own_kv = pltpu.make_async_copy(
        kvs.at[:, :, cols(hd)], kv.at[:, own_rows(me * m + hd, rows), :], loc_sem.at[5]
    )
    own_kv.start()
    own = pltpu.make_async_copy(
        stage.at[:, :, cols(me)], lin_all.at[:, own_rows(me, span), :], loc_sem.at[8]
    )
    own.start()
    pl.semaphore_wait(barrier, n + m - 2)

    def remote(src, dst, send, recv, device):
        return pltpu.make_async_remote_copy(
            src_ref=src, dst_ref=dst, send_sem=send, recv_sem=recv,
            device_id=device, device_id_type=MESH,
        )

    kv1, qsc = [], []
    for j, peer in enumerate(head_peers):
        kv1.append(
            remote(
                kvs.at[:, :, cols(peer)], kv.at[:, own_rows(me * m + hd, rows), :],
                kv1_s.at[j], kv1_r.at[j], {"head": peer},
            )
        )
        qsc.append(
            remote(
                qs_in.at[:, cols(peer, heads * DH)], qs.at[own_rows(hd, rows), :],
                qs_s.at[j], qs_r.at[j], {"head": peer},
            )
        )
    auxc = [
        remote(aux, aux_all.at[me], aux_s.at[j], aux_r.at[me], {"seq": peer})
        for j, peer in enumerate(seq_peers)
    ]
    linc = [
        remote(
            stage.at[:, :, cols(peer)], lin_all.at[:, own_rows(me, span), :],
            lin_s.at[j], lin_r.at[me], {"seq": peer},
        )
        for j, peer in enumerate(seq_peers)
    ]
    mine = kv.at[:, own_rows(me, span), :]
    kv2 = [
        remote(mine, mine, kv2_s.at[j], kv2_r.at[me], {"seq": peer})
        for j, peer in enumerate(seq_peers)
    ]

    def result_to(block):
        return remote(
            lin_v.at[block * span : (block + 1) * span, :], lin_out.at[:, cols(me)],
            out_s.at[block], out_r.at[me], {"seq": block},
        )

    def arrived(copy_from, source):
        @pl.when(source != me)
        def _():
            copy_from(source).wait_recv()

    def aux_from(source):
        return remote(aux, aux_all.at[source], aux_s.at[0], aux_r.at[source], {"seq": source})

    def lin_from(source):
        here = lin_all.at[:, source * span : (source + 1) * span, :]
        return remote(here, here, lin_s.at[0], lin_r.at[source], {"seq": source})

    def out_from(source):
        here = lin_out.at[:, source * DH : (source + 1) * DH]
        return remote(here, here, out_s.at[0], out_r.at[source], {"seq": source})

    for copy in kv1:
        copy.start()
    for small, large in zip(auxc, linc):
        small.start()
        large.start()
    for copy in qsc:
        copy.start()
    own_kv.wait()
    for copy in kv1:
        copy.wait_recv()
    for copy, peer in zip(kv2, seq_peers):
        pl.when(peer > me)(copy.start)

    def iota(shape, dim):
        return lax.broadcasted_iota(jnp.int32, shape, dim)

    eye_s = iota((span, span), 0) == iota((span, span), 1)
    doc_col = jnp.sum(jnp.where(eye_s, doc_v[...].astype(jnp.float32), 0.0), axis=1, keepdims=True)
    place = me * span + iota((span, tokens), 0)
    key_at = iota((span, tokens), 1)
    open_s = (key_at <= place) & (key_at >= doc_col.astype(jnp.int32))
    half = jnp.where(open_s, 0.0, masked_score)
    bias[0:span, :] = half
    bias[span : 2 * span, :] = half

    for source in range(n):
        arrived(aux_from, source)
    blk = 2 * span
    eye = iota((blk, blk), 0) == iota((blk, blk), 1)
    tri = iota((blk, blk), 0) >= iota((blk, blk), 1)
    sum_col, sum_row, doc_cols = [], [], []
    before = jnp.zeros((1, 1), jnp.float32)
    for i in range(tokens // blk):
        decay = jnp.concatenate(
            [aux_all[2 * i + b, pl.ds(me, 1), 0:span] for b in range(2)], axis=1
        )
        docs = jnp.concatenate(
            [aux_all[2 * i + b, heads : heads + 1, 0:span] for b in range(2)], axis=1
        )
        column = jnp.sum(jnp.where(tri, decay, 0.0), axis=1, keepdims=True) + before
        before = before + jnp.sum(decay, axis=1, keepdims=True)
        sum_col.append(column)
        sum_row.append(jnp.sum(jnp.where(eye, column, 0.0), axis=0, keepdims=True))
        doc_cols.append(jnp.sum(jnp.where(eye, docs, 0.0), axis=1, keepdims=True).astype(jnp.int32))

    own.wait()
    for i in range(tokens // blk):
        arrived(lin_from, 2 * i)
        arrived(lin_from, 2 * i + 1)
        here = slice(i * blk, (i + 1) * blk)
        reach = (i + 1) * blk
        score = lax.dot_general(
            lin_all[0, here, :], lin_all[1, 0:reach, :], NT, preferred_element_type=jnp.float32
        )
        gap = sum_col[i] - jnp.concatenate(sum_row[: i + 1], axis=1)
        at = iota((blk, reach), 1)
        is_open = (at >= doc_cols[i]) & (at <= i * blk + iota((blk, reach), 0))
        mix = jnp.where(is_open, score * jnp.exp(gap), 0.0)
        high = mix.astype(jnp.bfloat16)
        low = (mix - high.astype(jnp.float32)).astype(jnp.bfloat16)
        values = lin_all[2, 0:reach, :]
        out = jnp.dot(high, values, preferred_element_type=jnp.float32) + jnp.dot(
            low, values, preferred_element_type=jnp.float32
        )
        normed = out * lax.rsqrt(jnp.mean(out * out, axis=1, keepdims=True) + 1e-06)
        lin_v[here, :] = normed.astype(jnp.bfloat16)
        for block in (2 * i, 2 * i + 1):
            pl.when(block != me)(result_to(block).start)
    own_out = pltpu.make_async_copy(
        lin_v.at[own_rows(me, span), :], lin_out.at[:, cols(me)], loc_sem.at[9]
    )
    own_out.start()

    loads[7].wait()
    for copy in qsc:
        copy.wait_recv()
    for source in range(n - 1):

        @pl.when(source < me)
        def _():
            here = kv.at[:, source * span : (source + 1) * span, :]
            remote(here, here, kv2_s.at[0], kv2_r.at[source], {"seq": source}).wait_recv()

    stores = []
    for i in range(heads // 2):
        queries = jnp.concatenate(
            [qs[:, g * DH : (g + 1) * DH] for g in (2 * i, 2 * i + 1)], axis=0
        )
        score = lax.dot_general(queries, kv[0], NT, preferred_element_type=jnp.float32)
        score = score * DH ** (-0.5) + bias[...]
        top = jnp.max(score, axis=1, keepdims=True)
        weight = jnp.exp(score - top)
        total = jnp.sum(weight, axis=1, keepdims=True)
        out = jnp.dot(weight.astype(jnp.bfloat16), kv[1], preferred_element_type=jnp.float32)
        out = (out / total).astype(jnp.bfloat16)
        lse = top + jnp.log(total)
        for b in range(2):
            g = 2 * i + b
            part = slice(b * span, (b + 1) * span)
            soft_v[:, g * DH : (g + 1) * DH] = out[part]
            lse_v[g : g + 1, :] = jnp.sum(
                jnp.where(eye_s, lse[part], 0.0), axis=0, keepdims=True
            )
        pair = slice(2 * i * DH, 2 * (i + 1) * DH)
        stores.append(
            pltpu.make_async_copy(soft_v.at[:, pair], soft_out.at[:, pair], loc_sem.at[10 + i])
        )
        stores[-1].start()
    stores.append(pltpu.make_async_copy(lse_v, lse_out, loc_sem.at[10 + heads // 2]))
    stores[-1].start()

    for source in range(n):
        arrived(out_from, source)
    own_out.wait()
    for copy in stores:
        copy.wait()
    for copy in kv1 + auxc + linc + qsc:
        copy.wait_send()
    for copy, peer in zip(kv2, seq_peers):
        pl.when(peer > me)(copy.wait_send)
    for block in range(n):
        pl.when(block != me)(result_to(block).wait_send)


def fused(n, m, query_lin, key_lin, value_lin, log_decay, query_soft, key_soft, value_soft, doc_start):
    span, heads = query_lin.shape[0], log_decay.shape[0]
    tokens, rows = n * span, query_soft.shape[0]
    bf16, f32 = jnp.bfloat16, jnp.float32
    any_spec = pl.BlockSpec(memory_space=pl.ANY)
    hbm_spec = pl.BlockSpec(memory_space=pltpu.HBM)
    dma = pltpu.SemaphoreType.DMA
    results = pl.pallas_call(
        functools.partial(fused_kernel, n, m),
        out_shape=(
            jax.ShapeDtypeStruct((span, heads * DH), bf16),
            jax.ShapeDtypeStruct((span, heads * DH), bf16),
            jax.ShapeDtypeStruct((heads, span), f32),
        ),
        in_specs=[any_spec] * 8,
        out_specs=(any_spec,) * 3,
        scratch_shapes=[
            pltpu.VMEM((3, span, heads * DH), bf16),
            pltpu.VMEM((3, tokens, DH), bf16),
            pltpu.VMEM((2 * heads, DH), f32),
            pltpu.VMEM((n, 2 * heads, DH), f32),
            pltpu.VMEM((heads, span), f32),
            pltpu.VMEM((1, span), jnp.int32),
            pltpu.VMEM((span, heads * DH), bf16),
            pltpu.VMEM((2, rows, m * DH), bf16),
            pltpu.VMEM((2, tokens, DH), bf16),
            pltpu.VMEM((tokens, DH), bf16),
            pltpu.VMEM((span, heads * DH), bf16),
            pltpu.VMEM((heads, span), f32),
            pltpu.VMEM((2 * span, tokens), f32),
            dma((11 + heads // 2,)),
        ]
        + [dma((n,))] * 4
        + [dma((m - 1,))] * 4
        + [dma((n,))] * 4,
        compiler_params=pltpu.CompilerParams(
            collective_id=0, has_side_effects=True, vmem_limit_bytes=32 * 1024 * 1024
        ),
    )(*(pltpu.with_memory_space_constraint(x, pltpu.HBM) for x in (
        query_lin, key_lin, value_lin, log_decay, query_soft, key_soft, value_soft,
        doc_start.reshape(1, span),
    )))
    return pl.pallas_call(
        store_kernel,
        out_shape=tuple(jax.ShapeDtypeStruct(part.shape, part.dtype) for part in results),
        in_specs=[any_spec] * 3,
        out_specs=(hbm_spec,) * 3,
        scratch_shapes=[dma((3,))],
    )(*(pltpu.with_memory_space_constraint(part, pltpu.VMEM) for part in results))


def store_kernel(a, b, c, a_out, b_out, c_out, sem):
    copies = [
        pltpu.make_async_copy(src, dst, sem.at[i])
        for i, (src, dst) in enumerate(((a, a_out), (b, b_out), (c, c_out)))
    ]
    for copy in copies:
        copy.start()
    for copy in copies:
        copy.wait()


def per_device(
    query_lin, key_lin, value_lin, log_decay, query_soft, key_soft, value_soft, doc_start
):
    n, m = lax.axis_size("seq"), lax.axis_size("head")
    span, heads = query_lin.shape[0], log_decay.shape[0]
    if heads == n == 8 and span == DH // 2 and key_soft.shape[1] == m * DH:
        return fused(
            n, m, query_lin, key_lin, value_lin, log_decay,
            query_soft, key_soft, value_soft, doc_start,
        )
    lin_out = lightning_part(query_lin, key_lin, value_lin, log_decay, doc_start)
    soft_out, soft_lse = softmax_part(query_soft, key_soft, value_soft, doc_start)
    return (lin_out, soft_out, soft_lse)


def solution(mesh):
    return jax.shard_map(
        per_device,
        mesh=mesh,
        in_specs=(
            P("seq", "head"),
            P("seq", "head"),
            P("seq", "head"),
            P("head", "seq"),
            P(("seq", "head"), None),
            P(("seq", "head"), None),
            P(("seq", "head"), None),
            P("seq"),
        ),
        out_specs=(P("seq", "head"), P("seq", "head"), P("head", "seq")),
        check_vma=False,
    )
```

```python
import functools

import jax
import jax.numpy as jnp
from jax import lax
from jax.experimental import pallas as pl
from jax.experimental.pallas import tpu as pltpu
from jax.sharding import PartitionSpec as P


DH = 128


HIGHEST = lax.Precision.HIGHEST
masked_score = -1e30


def prefix(array, axis, combine, identity):
    size, here = (lax.axis_size(axis), lax.axis_index(axis))
    everything = jax.tree.map(lambda part: lax.all_gather(part, axis), array)
    start = jax.tree.map(
        lambda part, zero: jnp.broadcast_to(jnp.asarray(zero, part.dtype), part.shape),
        array,
        identity,
    )

    def lap(k, before):
        reached = k < here
        new = combine(before, jax.tree.map(lambda part: part[k], everything))
        return jax.tree.map(lambda a, b: jnp.where(reached, a, b), new, before)

    return lax.fori_loop(0, size, lap, start)


def span_terms(query_heads, key_heads, value_heads, decay_rows, doc_rows, first_place):
    span_len = query_heads.shape[0]
    cumulative = jnp.cumsum(decay_rows, axis=1)
    totals = cumulative[:, -1]
    token_positions = first_place + jnp.arange(span_len, dtype=jnp.int32)
    allowed = (token_positions[None, :] <= token_positions[:, None]) & (
        doc_rows[:, None] <= token_positions[None, :]
    )
    decay_gap = jnp.where(allowed[None], cumulative[:, :, None] - cumulative[:, None, :], 0.0)
    decay_mat = jnp.where(allowed[None], jnp.exp(decay_gap), 0.0)
    scores = jnp.einsum("thd,shd->hts", query_heads, key_heads, preferred_element_type=jnp.float32)
    key_float = key_heads.astype(jnp.float32)
    value_float = value_heads.astype(jnp.float32)
    inner_part = jnp.einsum("hts,shd->thd", scores * decay_mat, value_float, precision=HIGHEST)
    keep_mask = (doc_rows == doc_rows[-1]).astype(jnp.float32)
    tail_weight = jnp.exp(totals[:, None] - cumulative) * keep_mask[None, :]
    weighted_keys = key_float * jnp.transpose(tail_weight)[:, :, None]
    fresh_state = jnp.einsum("shd,she->hde", weighted_keys, value_float, precision=HIGHEST)
    carry_on = (doc_rows[-1] < first_place).astype(jnp.float32)
    factor = jnp.exp(totals) * carry_on
    read_mask = (doc_rows < first_place).astype(jnp.float32)[:, None] * jnp.transpose(
        jnp.exp(cumulative)
    )
    return (inner_part, fresh_state, factor, read_mask)


def combine_states(earlier, later_part):
    return (earlier[0] * later_part[0], later_part[0][:, None, None] * earlier[1] + later_part[1])


def lightning_part(query_lin, key_lin, value_lin, log_decay, doc_start):
    span_len = query_lin.shape[0]
    head_count = log_decay.shape[0]
    first_place = lax.axis_index("seq") * span_len
    query_heads = query_lin.reshape(span_len, head_count, DH)
    key_heads = key_lin.reshape(span_len, head_count, DH)
    value_heads = value_lin.reshape(span_len, head_count, DH)
    inner_part, fresh_state, factor, read_mask = span_terms(
        query_heads, key_heads, value_heads, log_decay, doc_start, first_place
    )
    identity = (jnp.ones((head_count,), jnp.float32), jnp.zeros((head_count, DH, DH), jnp.float32))
    unused, carried = prefix((factor, fresh_state), "seq", combine_states, identity)
    outer_part = (
        jnp.einsum("thd,hde->the", query_heads.astype(jnp.float32), carried, precision=HIGHEST)
        * read_mask[:, :, None]
    )
    mixed_out = inner_part + outer_part
    normed = mixed_out * lax.rsqrt(jnp.mean(mixed_out * mixed_out, axis=-1, keepdims=True) + 1e-06)
    return normed.astype(jnp.bfloat16).reshape(span_len, head_count * DH)


def softmax_part(query_soft, key_soft, value_soft, doc_start):
    queries, keys_local, values_local = (
        lax.all_to_all(query_soft, "head", split_axis=1, concat_axis=0, tiled=True),
        lax.all_to_all(key_soft, "head", split_axis=1, concat_axis=0, tiled=True),
        lax.all_to_all(value_soft, "head", split_axis=1, concat_axis=0, tiled=True),
    )
    span_len = queries.shape[0]
    kv_count = keys_local.shape[1] // DH
    group_size = queries.shape[1] // keys_local.shape[1]
    first_place = lax.axis_index("seq") * span_len
    query_places = first_place + jnp.arange(span_len, dtype=jnp.int32)
    query_heads = queries.reshape(span_len, kv_count, group_size, DH)
    score_scale = DH ** (-0.5)
    start_state = (
        jnp.full((span_len, kv_count, group_size), masked_score, jnp.float32),
        jnp.zeros((span_len, kv_count, group_size), jnp.float32),
        jnp.zeros((span_len, kv_count, group_size, DH), jnp.float32),
    )
    key_piece = lax.all_gather(keys_local, "seq", axis=0, tiled=True)
    value_piece = lax.all_gather(values_local, "seq", axis=0, tiled=True)
    piece_rows = key_piece.shape[0]
    block_rows = max(
        (divisor for divisor in range(1, min(piece_rows, 1024) + 1) if piece_rows % divisor == 0)
    )
    block_count = piece_rows // block_rows
    key_parts = key_piece.reshape(block_count, block_rows, kv_count, DH)
    value_parts = value_piece.reshape(block_count, block_rows, kv_count, DH)
    begin_rows = jnp.int32(0) + block_rows * jnp.arange(block_count, dtype=jnp.int32)

    def absorb_block(running, slices):
        key_block, value_block, begin_row = slices
        running_max, norm_sum, accum_out = running
        token_positions = begin_row + jnp.arange(block_rows, dtype=jnp.int32)
        allowed = (token_positions[None, :] <= query_places[:, None]) & (
            doc_start[:, None] <= token_positions[None, :]
        )
        allowed = allowed[:, None, None, :]
        scores = (
            jnp.einsum("tkgd,skd->tkgs", query_heads, key_block, preferred_element_type=jnp.float32)
            * score_scale
        )
        new_max = jnp.maximum(
            running_max, jnp.max(jnp.where(allowed, scores, masked_score), axis=-1)
        )
        raw_weight = jnp.where(allowed, jnp.exp(scores - new_max[..., None]), 0.0)
        shrink = jnp.exp(running_max - new_max)
        norm_sum = norm_sum * shrink + jnp.sum(raw_weight, axis=-1)
        accum_out = accum_out * shrink[..., None] + jnp.einsum(
            "tkgs,skd->tkgd",
            raw_weight.astype(jnp.bfloat16),
            value_block,
            preferred_element_type=jnp.float32,
        )
        running = (new_max, norm_sum, accum_out)
        return (running, None)

    final_state, unused = lax.scan(absorb_block, start_state, (key_parts, value_parts, begin_rows))
    running_max, norm_sum, accum_out = final_state
    soft_out = (
        (accum_out / norm_sum[..., None])
        .astype(jnp.bfloat16)
        .reshape(span_len, kv_count * group_size * DH)
    )
    soft_lse = jnp.transpose(
        (running_max + jnp.log(norm_sum)).reshape(span_len, kv_count * group_size)
    )
    return (soft_out, soft_lse)


MESH = pl.DeviceIdType.MESH
NT = (((1,), (1,)), ((), ()))


def fused_kernel(
    n, m, q_in, k_in, v_in, ld_in, qs_in, ks_in, vs_in, doc_in,
    lin_out, soft_out, lse_out,
    stage, lin_all, aux, aux_all, ld_v, doc_v, qs, kvs, kv, lin_v, soft_v, lse_v, bias,
    loc_sem, lin_s, lin_r, aux_s, aux_r, kv1_s, kv1_r, qs_s, qs_r, kv2_s, kv2_r, out_s, out_r,
):
    span, heads = doc_in.shape[1], ld_in.shape[0]
    rows = qs_in.shape[0]
    tokens = n * span
    me, hd = lax.axis_index("seq"), lax.axis_index("head")

    kv[...] = jnp.zeros_like(kv)
    barrier = pltpu.get_barrier_semaphore()
    pair, core = me // 2, lax.rem(me, 2)
    far = [n // 2 - 1 - pair, pair + 1 - 2 * lax.rem(pair, 2)]
    far += [lax.rem(pair + j, n // 2) for j in range(2, n // 2, 2)]
    seq_peers = [2 * other + c for other in far for c in (core, 1 - core)] + [me + 1 - 2 * core]
    head_peers = [lax.rem(hd + j, m) for j in range(1, m)]
    for peer in head_peers:
        pl.semaphore_signal(barrier, inc=1, device_id={"head": peer}, device_id_type=MESH)
    for peer in seq_peers:
        pl.semaphore_signal(barrier, inc=1, device_id={"seq": peer}, device_id_type=MESH)

    def cols(index, width=DH):
        return pl.ds(pl.multiple_of(index * width, width), width)

    def own_rows(index, count):
        return pl.ds(pl.multiple_of(index * count, count), count)

    loads = [
        pltpu.make_async_copy(ld_in, ld_v, loc_sem.at[0]),
        pltpu.make_async_copy(doc_in, doc_v, loc_sem.at[1]),
        pltpu.make_async_copy(q_in, stage.at[0], loc_sem.at[2]),
        pltpu.make_async_copy(k_in, stage.at[1], loc_sem.at[3]),
        pltpu.make_async_copy(v_in, stage.at[2], loc_sem.at[4]),
        pltpu.make_async_copy(ks_in, kvs.at[0], loc_sem.at[5]),
        pltpu.make_async_copy(vs_in, kvs.at[1], loc_sem.at[6]),
        pltpu.make_async_copy(
            qs_in.at[:, cols(hd, heads * DH)], qs.at[own_rows(hd, rows), :], loc_sem.at[7]
        ),
    ]
    for load in loads:
        load.start()
    aux[...] = jnp.zeros_like(aux)
    loads[0].wait()
    loads[1].wait()
    aux[0:heads, 0:span] = ld_v[...]
    aux[heads : heads + 1, 0:span] = doc_v[...].astype(jnp.float32)
    aux_all[me] = aux[...]
    for load in loads[2:7]:
        load.wait()
    own_kv = pltpu.make_async_copy(
        kvs.at[:, :, cols(hd)], kv.at[:, own_rows(me * m + hd, rows), :], loc_sem.at[5]
    )
    own_kv.start()
    own = pltpu.make_async_copy(
        stage.at[:, :, cols(me)], lin_all.at[:, own_rows(me, span), :], loc_sem.at[8]
    )
    own.start()
    pl.semaphore_wait(barrier, n + m - 2)

    def remote(src, dst, send, recv, device):
        return pltpu.make_async_remote_copy(
            src_ref=src, dst_ref=dst, send_sem=send, recv_sem=recv,
            device_id=device, device_id_type=MESH,
        )

    kv1, qsc = [], []
    for j, peer in enumerate(head_peers):
        kv1.append(
            remote(
                kvs.at[:, :, cols(peer)], kv.at[:, own_rows(me * m + hd, rows), :],
                kv1_s.at[j], kv1_r.at[j], {"head": peer},
            )
        )
        qsc.append(
            remote(
                qs_in.at[:, cols(peer, heads * DH)], qs.at[own_rows(hd, rows), :],
                qs_s.at[j], qs_r.at[j], {"head": peer},
            )
        )
    auxc = [
        remote(aux, aux_all.at[me], aux_s.at[j], aux_r.at[me], {"seq": peer})
        for j, peer in enumerate(seq_peers)
    ]
    linc = [
        remote(
            stage.at[:, :, cols(peer)], lin_all.at[:, own_rows(me, span), :],
            lin_s.at[j], lin_r.at[me], {"seq": peer},
        )
        for j, peer in enumerate(seq_peers)
    ]
    mine = kv.at[:, own_rows(me, span), :]
    kv2 = [
        remote(mine, mine, kv2_s.at[j], kv2_r.at[me], {"seq": peer})
        for j, peer in enumerate(seq_peers)
    ]

    def result_to(block):
        return remote(
            lin_v.at[block * span : (block + 1) * span, :], lin_out.at[:, cols(me)],
            out_s.at[block], out_r.at[me], {"seq": block},
        )

    def arrived(copy_from, source):
        @pl.when(source != me)
        def _():
            copy_from(source).wait_recv()

    def aux_from(source):
        return remote(aux, aux_all.at[source], aux_s.at[0], aux_r.at[source], {"seq": source})

    def lin_from(source):
        here = lin_all.at[:, source * span : (source + 1) * span, :]
        return remote(here, here, lin_s.at[0], lin_r.at[source], {"seq": source})

    def out_from(source):
        here = lin_out.at[:, source * DH : (source + 1) * DH]
        return remote(here, here, out_s.at[0], out_r.at[source], {"seq": source})

    for copy in auxc + kv1 + linc + qsc:
        copy.start()
    own_kv.wait()
    for copy in kv1:
        copy.wait_recv()
    for copy, peer in zip(kv2, seq_peers):
        pl.when(peer > me)(copy.start)

    def iota(shape, dim):
        return lax.broadcasted_iota(jnp.int32, shape, dim)

    eye_s = iota((span, span), 0) == iota((span, span), 1)
    doc_col = jnp.sum(jnp.where(eye_s, doc_v[...].astype(jnp.float32), 0.0), axis=1, keepdims=True)
    place = me * span + iota((span, tokens), 0)
    key_at = iota((span, tokens), 1)
    open_s = (key_at <= place) & (key_at >= doc_col.astype(jnp.int32))
    half = jnp.where(open_s, 0.0, masked_score)
    bias[0:span, :] = half
    bias[span : 2 * span, :] = half

    for source in range(n):
        arrived(aux_from, source)
    blk = 2 * span
    eye = iota((blk, blk), 0) == iota((blk, blk), 1)
    tri = iota((blk, blk), 0) >= iota((blk, blk), 1)
    sum_col, sum_row, doc_cols = [], [], []
    before = jnp.zeros((1, 1), jnp.float32)
    for i in range(tokens // blk):
        decay = jnp.concatenate(
            [aux_all[2 * i + b, pl.ds(me, 1), 0:span] for b in range(2)], axis=1
        )
        docs = jnp.concatenate(
            [aux_all[2 * i + b, heads : heads + 1, 0:span] for b in range(2)], axis=1
        )
        column = jnp.sum(jnp.where(tri, decay, 0.0), axis=1, keepdims=True) + before
        before = before + jnp.sum(decay, axis=1, keepdims=True)
        sum_col.append(column)
        sum_row.append(jnp.sum(jnp.where(eye, column, 0.0), axis=0, keepdims=True))
        doc_cols.append(jnp.sum(jnp.where(eye, docs, 0.0), axis=1, keepdims=True).astype(jnp.int32))

    own.wait()
    for i in range(tokens // blk):
        arrived(lin_from, 2 * i)
        arrived(lin_from, 2 * i + 1)
        here = slice(i * blk, (i + 1) * blk)
        reach = (i + 1) * blk
        score = lax.dot_general(
            lin_all[0, here, :], lin_all[1, 0:reach, :], NT, preferred_element_type=jnp.float32
        )
        gap = sum_col[i] - jnp.concatenate(sum_row[: i + 1], axis=1)
        at = iota((blk, reach), 1)
        is_open = (at >= doc_cols[i]) & (at <= i * blk + iota((blk, reach), 0))
        mix = jnp.where(is_open, score * jnp.exp(gap), 0.0)
        high = mix.astype(jnp.bfloat16)
        low = (mix - high.astype(jnp.float32)).astype(jnp.bfloat16)
        values = lin_all[2, 0:reach, :]
        out = jnp.dot(high, values, preferred_element_type=jnp.float32) + jnp.dot(
            low, values, preferred_element_type=jnp.float32
        )
        normed = out * lax.rsqrt(jnp.mean(out * out, axis=1, keepdims=True) + 1e-06)
        lin_v[here, :] = normed.astype(jnp.bfloat16)
        for block in (2 * i, 2 * i + 1):
            pl.when(block != me)(result_to(block).start)
    own_out = pltpu.make_async_copy(
        lin_v.at[own_rows(me, span), :], lin_out.at[:, cols(me)], loc_sem.at[9]
    )
    own_out.start()

    loads[7].wait()
    for copy in qsc:
        copy.wait_recv()
    for source in range(n - 1):

        @pl.when(source < me)
        def _():
            here = kv.at[:, source * span : (source + 1) * span, :]
            remote(here, here, kv2_s.at[0], kv2_r.at[source], {"seq": source}).wait_recv()

    stores = []
    for i in range(heads // 2):
        queries = jnp.concatenate(
            [qs[:, g * DH : (g + 1) * DH] for g in (2 * i, 2 * i + 1)], axis=0
        )
        score = lax.dot_general(queries, kv[0], NT, preferred_element_type=jnp.float32)
        score = score * DH ** (-0.5) + bias[...]
        top = jnp.max(score, axis=1, keepdims=True)
        weight = jnp.exp(score - top)
        total = jnp.sum(weight, axis=1, keepdims=True)
        out = jnp.dot(weight.astype(jnp.bfloat16), kv[1], preferred_element_type=jnp.float32)
        out = (out / total).astype(jnp.bfloat16)
        lse = top + jnp.log(total)
        for b in range(2):
            g = 2 * i + b
            part = slice(b * span, (b + 1) * span)
            soft_v[:, g * DH : (g + 1) * DH] = out[part]
            lse_v[g : g + 1, :] = jnp.sum(
                jnp.where(eye_s, lse[part], 0.0), axis=0, keepdims=True
            )
        pair = slice(2 * i * DH, 2 * (i + 1) * DH)
        stores.append(
            pltpu.make_async_copy(soft_v.at[:, pair], soft_out.at[:, pair], loc_sem.at[10 + i])
        )
        stores[-1].start()
    stores.append(pltpu.make_async_copy(lse_v, lse_out, loc_sem.at[10 + heads // 2]))
    stores[-1].start()

    for copy in kv1 + auxc + linc + qsc:
        copy.wait_send()
    for copy, peer in zip(kv2, seq_peers):
        pl.when(peer > me)(copy.wait_send)
    for block in range(n):
        pl.when(block != me)(result_to(block).wait_send)
    for source in range(n):
        arrived(out_from, source)
    own_out.wait()
    for copy in stores:
        copy.wait()


def fused(n, m, query_lin, key_lin, value_lin, log_decay, query_soft, key_soft, value_soft, doc_start):
    span, heads = query_lin.shape[0], log_decay.shape[0]
    tokens, rows = n * span, query_soft.shape[0]
    bf16, f32 = jnp.bfloat16, jnp.float32
    any_spec = pl.BlockSpec(memory_space=pl.ANY)
    hbm_spec = pl.BlockSpec(memory_space=pltpu.HBM)
    dma = pltpu.SemaphoreType.DMA
    results = pl.pallas_call(
        functools.partial(fused_kernel, n, m),
        out_shape=(
            jax.ShapeDtypeStruct((span, heads * DH), bf16),
            jax.ShapeDtypeStruct((span, heads * DH), bf16),
            jax.ShapeDtypeStruct((heads, span), f32),
        ),
        in_specs=[any_spec] * 8,
        out_specs=(any_spec,) * 3,
        scratch_shapes=[
            pltpu.VMEM((3, span, heads * DH), bf16),
            pltpu.VMEM((3, tokens, DH), bf16),
            pltpu.VMEM((2 * heads, DH), f32),
            pltpu.VMEM((n, 2 * heads, DH), f32),
            pltpu.VMEM((heads, span), f32),
            pltpu.VMEM((1, span), jnp.int32),
            pltpu.VMEM((span, heads * DH), bf16),
            pltpu.VMEM((2, rows, m * DH), bf16),
            pltpu.VMEM((2, tokens, DH), bf16),
            pltpu.VMEM((tokens, DH), bf16),
            pltpu.VMEM((span, heads * DH), bf16),
            pltpu.VMEM((heads, span), f32),
            pltpu.VMEM((2 * span, tokens), f32),
            dma((11 + heads // 2,)),
        ]
        + [dma((n,))] * 4
        + [dma((m - 1,))] * 4
        + [dma((n,))] * 4,
        compiler_params=pltpu.CompilerParams(
            collective_id=0, has_side_effects=True, vmem_limit_bytes=32 * 1024 * 1024
        ),
    )(*(pltpu.with_memory_space_constraint(x, pltpu.HBM) for x in (
        query_lin, key_lin, value_lin, log_decay, query_soft, key_soft, value_soft,
        doc_start.reshape(1, span),
    )))
    return pl.pallas_call(
        store_kernel,
        out_shape=tuple(jax.ShapeDtypeStruct(part.shape, part.dtype) for part in results),
        in_specs=[any_spec] * 3,
        out_specs=(hbm_spec,) * 3,
        scratch_shapes=[dma((3,))],
    )(*(pltpu.with_memory_space_constraint(part, pltpu.VMEM) for part in results))


def store_kernel(a, b, c, a_out, b_out, c_out, sem):
    copies = [
        pltpu.make_async_copy(src, dst, sem.at[i])
        for i, (src, dst) in enumerate(((a, a_out), (b, b_out), (c, c_out)))
    ]
    for copy in copies:
        copy.start()
    for copy in copies:
        copy.wait()


def per_device(
    query_lin, key_lin, value_lin, log_decay, query_soft, key_soft, value_soft, doc_start
):
    n, m = lax.axis_size("seq"), lax.axis_size("head")
    span, heads = query_lin.shape[0], log_decay.shape[0]
    if heads == n == 8 and span == DH // 2 and key_soft.shape[1] == m * DH:
        return fused(
            n, m, query_lin, key_lin, value_lin, log_decay,
            query_soft, key_soft, value_soft, doc_start,
        )
    lin_out = lightning_part(query_lin, key_lin, value_lin, log_decay, doc_start)
    soft_out, soft_lse = softmax_part(query_soft, key_soft, value_soft, doc_start)
    return (lin_out, soft_out, soft_lse)


def solution(mesh):
    return jax.shard_map(
        per_device,
        mesh=mesh,
        in_specs=(
            P("seq", "head"),
            P("seq", "head"),
            P("seq", "head"),
            P("head", "seq"),
            P(("seq", "head"), None),
            P(("seq", "head"), None),
            P(("seq", "head"), None),
            P("seq"),
        ),
        out_specs=(P("seq", "head"), P("seq", "head"), P("head", "seq")),
        check_vma=False,
    )
```

```python
import functools

import jax
import jax.numpy as jnp
from jax import lax
from jax.experimental import pallas as pl
from jax.experimental.pallas import tpu as pltpu
from jax.sharding import PartitionSpec as P


DH = 128


HIGHEST = lax.Precision.HIGHEST
masked_score = -1e30


def prefix(array, axis, combine, identity):
    size, here = (lax.axis_size(axis), lax.axis_index(axis))
    everything = jax.tree.map(lambda part: lax.all_gather(part, axis), array)
    start = jax.tree.map(
        lambda part, zero: jnp.broadcast_to(jnp.asarray(zero, part.dtype), part.shape),
        array,
        identity,
    )

    def lap(k, before):
        reached = k < here
        new = combine(before, jax.tree.map(lambda part: part[k], everything))
        return jax.tree.map(lambda a, b: jnp.where(reached, a, b), new, before)

    return lax.fori_loop(0, size, lap, start)


def span_terms(query_heads, key_heads, value_heads, decay_rows, doc_rows, first_place):
    span_len = query_heads.shape[0]
    cumulative = jnp.cumsum(decay_rows, axis=1)
    totals = cumulative[:, -1]
    token_positions = first_place + jnp.arange(span_len, dtype=jnp.int32)
    allowed = (token_positions[None, :] <= token_positions[:, None]) & (
        doc_rows[:, None] <= token_positions[None, :]
    )
    decay_gap = jnp.where(allowed[None], cumulative[:, :, None] - cumulative[:, None, :], 0.0)
    decay_mat = jnp.where(allowed[None], jnp.exp(decay_gap), 0.0)
    scores = jnp.einsum("thd,shd->hts", query_heads, key_heads, preferred_element_type=jnp.float32)
    key_float = key_heads.astype(jnp.float32)
    value_float = value_heads.astype(jnp.float32)
    inner_part = jnp.einsum("hts,shd->thd", scores * decay_mat, value_float, precision=HIGHEST)
    keep_mask = (doc_rows == doc_rows[-1]).astype(jnp.float32)
    tail_weight = jnp.exp(totals[:, None] - cumulative) * keep_mask[None, :]
    weighted_keys = key_float * jnp.transpose(tail_weight)[:, :, None]
    fresh_state = jnp.einsum("shd,she->hde", weighted_keys, value_float, precision=HIGHEST)
    carry_on = (doc_rows[-1] < first_place).astype(jnp.float32)
    factor = jnp.exp(totals) * carry_on
    read_mask = (doc_rows < first_place).astype(jnp.float32)[:, None] * jnp.transpose(
        jnp.exp(cumulative)
    )
    return (inner_part, fresh_state, factor, read_mask)


def combine_states(earlier, later_part):
    return (earlier[0] * later_part[0], later_part[0][:, None, None] * earlier[1] + later_part[1])


def lightning_part(query_lin, key_lin, value_lin, log_decay, doc_start):
    span_len = query_lin.shape[0]
    head_count = log_decay.shape[0]
    first_place = lax.axis_index("seq") * span_len
    query_heads = query_lin.reshape(span_len, head_count, DH)
    key_heads = key_lin.reshape(span_len, head_count, DH)
    value_heads = value_lin.reshape(span_len, head_count, DH)
    inner_part, fresh_state, factor, read_mask = span_terms(
        query_heads, key_heads, value_heads, log_decay, doc_start, first_place
    )
    identity = (jnp.ones((head_count,), jnp.float32), jnp.zeros((head_count, DH, DH), jnp.float32))
    unused, carried = prefix((factor, fresh_state), "seq", combine_states, identity)
    outer_part = (
        jnp.einsum("thd,hde->the", query_heads.astype(jnp.float32), carried, precision=HIGHEST)
        * read_mask[:, :, None]
    )
    mixed_out = inner_part + outer_part
    normed = mixed_out * lax.rsqrt(jnp.mean(mixed_out * mixed_out, axis=-1, keepdims=True) + 1e-06)
    return normed.astype(jnp.bfloat16).reshape(span_len, head_count * DH)


def softmax_part(query_soft, key_soft, value_soft, doc_start):
    queries, keys_local, values_local = (
        lax.all_to_all(query_soft, "head", split_axis=1, concat_axis=0, tiled=True),
        lax.all_to_all(key_soft, "head", split_axis=1, concat_axis=0, tiled=True),
        lax.all_to_all(value_soft, "head", split_axis=1, concat_axis=0, tiled=True),
    )
    span_len = queries.shape[0]
    kv_count = keys_local.shape[1] // DH
    group_size = queries.shape[1] // keys_local.shape[1]
    first_place = lax.axis_index("seq") * span_len
    query_places = first_place + jnp.arange(span_len, dtype=jnp.int32)
    query_heads = queries.reshape(span_len, kv_count, group_size, DH)
    score_scale = DH ** (-0.5)
    start_state = (
        jnp.full((span_len, kv_count, group_size), masked_score, jnp.float32),
        jnp.zeros((span_len, kv_count, group_size), jnp.float32),
        jnp.zeros((span_len, kv_count, group_size, DH), jnp.float32),
    )
    key_piece = lax.all_gather(keys_local, "seq", axis=0, tiled=True)
    value_piece = lax.all_gather(values_local, "seq", axis=0, tiled=True)
    piece_rows = key_piece.shape[0]
    block_rows = max(
        (divisor for divisor in range(1, min(piece_rows, 1024) + 1) if piece_rows % divisor == 0)
    )
    block_count = piece_rows // block_rows
    key_parts = key_piece.reshape(block_count, block_rows, kv_count, DH)
    value_parts = value_piece.reshape(block_count, block_rows, kv_count, DH)
    begin_rows = jnp.int32(0) + block_rows * jnp.arange(block_count, dtype=jnp.int32)

    def absorb_block(running, slices):
        key_block, value_block, begin_row = slices
        running_max, norm_sum, accum_out = running
        token_positions = begin_row + jnp.arange(block_rows, dtype=jnp.int32)
        allowed = (token_positions[None, :] <= query_places[:, None]) & (
            doc_start[:, None] <= token_positions[None, :]
        )
        allowed = allowed[:, None, None, :]
        scores = (
            jnp.einsum("tkgd,skd->tkgs", query_heads, key_block, preferred_element_type=jnp.float32)
            * score_scale
        )
        new_max = jnp.maximum(
            running_max, jnp.max(jnp.where(allowed, scores, masked_score), axis=-1)
        )
        raw_weight = jnp.where(allowed, jnp.exp(scores - new_max[..., None]), 0.0)
        shrink = jnp.exp(running_max - new_max)
        norm_sum = norm_sum * shrink + jnp.sum(raw_weight, axis=-1)
        accum_out = accum_out * shrink[..., None] + jnp.einsum(
            "tkgs,skd->tkgd",
            raw_weight.astype(jnp.bfloat16),
            value_block,
            preferred_element_type=jnp.float32,
        )
        running = (new_max, norm_sum, accum_out)
        return (running, None)

    final_state, unused = lax.scan(absorb_block, start_state, (key_parts, value_parts, begin_rows))
    running_max, norm_sum, accum_out = final_state
    soft_out = (
        (accum_out / norm_sum[..., None])
        .astype(jnp.bfloat16)
        .reshape(span_len, kv_count * group_size * DH)
    )
    soft_lse = jnp.transpose(
        (running_max + jnp.log(norm_sum)).reshape(span_len, kv_count * group_size)
    )
    return (soft_out, soft_lse)


MESH = pl.DeviceIdType.MESH
NT = (((1,), (1,)), ((), ()))


def fused_kernel(
    n, m, q_in, k_in, v_in, ld_in, qs_in, ks_in, vs_in, doc_in,
    lin_out, soft_out, lse_out,
    stage, lin_all, aux, aux_all, ld_v, doc_v, qs, kvs, kv, lin_v, soft_v, lse_v, bias,
    loc_sem, lin_s, lin_r, aux_s, aux_r, kv1_s, kv1_r, qs_s, qs_r, kv2_s, kv2_r, out_s, out_r,
):
    span, heads = doc_in.shape[1], ld_in.shape[0]
    rows = qs_in.shape[0]
    tokens = n * span
    me, hd = lax.axis_index("seq"), lax.axis_index("head")

    barrier = pltpu.get_barrier_semaphore()
    pair, core = me // 2, lax.rem(me, 2)
    far = [n // 2 - 1 - pair, pair + 1 - 2 * lax.rem(pair, 2)]
    far += [lax.rem(pair + j, n // 2) for j in range(2, n // 2, 2)]
    seq_peers = [2 * other + c for other in far for c in (core, 1 - core)] + [me + 1 - 2 * core]
    head_peers = [lax.rem(hd + j, m) for j in range(1, m)]
    for peer in head_peers:
        pl.semaphore_signal(barrier, inc=1, device_id={"head": peer}, device_id_type=MESH)
    for peer in seq_peers:
        pl.semaphore_signal(barrier, inc=1, device_id={"seq": peer}, device_id_type=MESH)

    def cols(index, width=DH):
        return pl.ds(pl.multiple_of(index * width, width), width)

    def own_rows(index, count):
        return pl.ds(pl.multiple_of(index * count, count), count)

    loads = [
        pltpu.make_async_copy(ld_in, ld_v, loc_sem.at[0]),
        pltpu.make_async_copy(doc_in, doc_v, loc_sem.at[1]),
        pltpu.make_async_copy(q_in, stage.at[0], loc_sem.at[2]),
        pltpu.make_async_copy(k_in, stage.at[1], loc_sem.at[3]),
        pltpu.make_async_copy(v_in, stage.at[2], loc_sem.at[4]),
        pltpu.make_async_copy(ks_in, kvs.at[0], loc_sem.at[5]),
        pltpu.make_async_copy(vs_in, kvs.at[1], loc_sem.at[6]),
        pltpu.make_async_copy(
            qs_in.at[:, cols(hd, heads * DH)], qs.at[own_rows(hd, rows), :], loc_sem.at[7]
        ),
    ]
    for load in loads:
        load.start()
    aux[...] = jnp.zeros_like(aux)
    loads[0].wait()
    loads[1].wait()
    aux[0:heads, 0:span] = ld_v[...]
    aux[heads : heads + 1, 0:span] = doc_v[...].astype(jnp.float32)
    aux_all[me] = aux[...]
    for block in range(1, n):

        @pl.when(block > me)
        def _():
            part = slice(block * span, (block + 1) * span)
            kv[:, part, :] = jnp.zeros((2, span, DH), kv.dtype)

    pl.semaphore_wait(barrier, n + m - 2)

    def remote(src, dst, send, recv, device):
        return pltpu.make_async_remote_copy(
            src_ref=src, dst_ref=dst, send_sem=send, recv_sem=recv,
            device_id=device, device_id_type=MESH,
        )

    kv1, qsc = [], []
    for j, peer in enumerate(head_peers):
        kv1.append(
            remote(
                kvs.at[:, :, cols(peer)], kv.at[:, own_rows(me * m + hd, rows), :],
                kv1_s.at[j], kv1_r.at[j], {"head": peer},
            )
        )
        qsc.append(
            remote(
                qs_in.at[:, cols(peer, heads * DH)], qs.at[own_rows(hd, rows), :],
                qs_s.at[j], qs_r.at[j], {"head": peer},
            )
        )
    auxc = [
        remote(aux, aux_all.at[me], aux_s.at[j], aux_r.at[me], {"seq": peer})
        for j, peer in enumerate(seq_peers)
    ]
    linc = [
        remote(
            stage.at[:, :, cols(peer)], lin_all.at[:, own_rows(me, span), :],
            lin_s.at[j], lin_r.at[me], {"seq": peer},
        )
        for j, peer in enumerate(seq_peers)
    ]
    mine = kv.at[:, own_rows(me, span), :]
    kv2 = [
        remote(mine, mine, kv2_s.at[j], kv2_r.at[me], {"seq": peer})
        for j, peer in enumerate(seq_peers)
    ]

    def result_to(block):
        return remote(
            lin_v.at[block * span : (block + 1) * span, :], lin_out.at[:, cols(me)],
            out_s.at[block], out_r.at[me], {"seq": block},
        )

    def arrived(copy_from, source):
        @pl.when(source != me)
        def _():
            copy_from(source).wait_recv()

    def aux_from(source):
        return remote(aux, aux_all.at[source], aux_s.at[0], aux_r.at[source], {"seq": source})

    def lin_from(source):
        here = lin_all.at[:, source * span : (source + 1) * span, :]
        return remote(here, here, lin_s.at[0], lin_r.at[source], {"seq": source})

    def out_from(source):
        here = lin_out.at[:, source * DH : (source + 1) * DH]
        return remote(here, here, out_s.at[0], out_r.at[source], {"seq": source})

    for copy in auxc:
        copy.start()
    for load in loads[2:7]:
        load.wait()
    own_kv = pltpu.make_async_copy(
        kvs.at[:, :, cols(hd)], kv.at[:, own_rows(me * m + hd, rows), :], loc_sem.at[5]
    )
    own_kv.start()
    own = pltpu.make_async_copy(
        stage.at[:, :, cols(me)], lin_all.at[:, own_rows(me, span), :], loc_sem.at[8]
    )
    own.start()
    for copy in kv1 + linc + qsc:
        copy.start()
    own_kv.wait()
    for copy in kv1:
        copy.wait_recv()
    for copy, peer in zip(kv2, seq_peers):
        pl.when(peer > me)(copy.start)

    def iota(shape, dim):
        return lax.broadcasted_iota(jnp.int32, shape, dim)

    eye_s = iota((span, span), 0) == iota((span, span), 1)
    doc_col = jnp.sum(jnp.where(eye_s, doc_v[...].astype(jnp.float32), 0.0), axis=1, keepdims=True)
    place = me * span + iota((span, tokens), 0)
    key_at = iota((span, tokens), 1)
    open_s = (key_at <= place) & (key_at >= doc_col.astype(jnp.int32))
    half = jnp.where(open_s, 0.0, masked_score)
    bias[0:span, :] = half
    bias[span : 2 * span, :] = half

    for source in range(n):
        arrived(aux_from, source)
    blk = 2 * span
    eye = iota((blk, blk), 0) == iota((blk, blk), 1)
    tri = iota((blk, blk), 0) >= iota((blk, blk), 1)
    sum_col, sum_row, doc_cols = [], [], []
    before = jnp.zeros((1, 1), jnp.float32)
    for i in range(tokens // blk):
        decay = jnp.concatenate(
            [aux_all[2 * i + b, pl.ds(me, 1), 0:span] for b in range(2)], axis=1
        )
        docs = jnp.concatenate(
            [aux_all[2 * i + b, heads : heads + 1, 0:span] for b in range(2)], axis=1
        )
        column = jnp.sum(jnp.where(tri, decay, 0.0), axis=1, keepdims=True) + before
        before = before + jnp.sum(decay, axis=1, keepdims=True)
        sum_col.append(column)
        sum_row.append(jnp.sum(jnp.where(eye, column, 0.0), axis=0, keepdims=True))
        doc_cols.append(jnp.sum(jnp.where(eye, docs, 0.0), axis=1, keepdims=True).astype(jnp.int32))

    own.wait()
    for i in range(tokens // blk):
        arrived(lin_from, 2 * i)
        arrived(lin_from, 2 * i + 1)
        here = slice(i * blk, (i + 1) * blk)
        reach = (i + 1) * blk
        score = lax.dot_general(
            lin_all[0, here, :], lin_all[1, 0:reach, :], NT, preferred_element_type=jnp.float32
        )
        gap = sum_col[i] - jnp.concatenate(sum_row[: i + 1], axis=1)
        at = iota((blk, reach), 1)
        is_open = (at >= doc_cols[i]) & (at <= i * blk + iota((blk, reach), 0))
        mix = jnp.where(is_open, score * jnp.exp(gap), 0.0)
        high = mix.astype(jnp.bfloat16)
        low = (mix - high.astype(jnp.float32)).astype(jnp.bfloat16)
        values = lin_all[2, 0:reach, :]
        out = jnp.dot(high, values, preferred_element_type=jnp.float32) + jnp.dot(
            low, values, preferred_element_type=jnp.float32
        )
        normed = out * lax.rsqrt(jnp.mean(out * out, axis=1, keepdims=True) + 1e-06)
        lin_v[here, :] = normed.astype(jnp.bfloat16)
        for block in (2 * i, 2 * i + 1):
            pl.when(block != me)(result_to(block).start)
    own_out = pltpu.make_async_copy(
        lin_v.at[own_rows(me, span), :], lin_out.at[:, cols(me)], loc_sem.at[9]
    )
    own_out.start()

    loads[7].wait()
    for copy in qsc:
        copy.wait_recv()
    for source in range(n - 1):

        @pl.when(source < me)
        def _():
            here = kv.at[:, source * span : (source + 1) * span, :]
            remote(here, here, kv2_s.at[0], kv2_r.at[source], {"seq": source}).wait_recv()

    stores = []
    for i in range(heads // 2):
        queries = jnp.concatenate(
            [qs[:, g * DH : (g + 1) * DH] for g in (2 * i, 2 * i + 1)], axis=0
        )
        score = lax.dot_general(queries, kv[0], NT, preferred_element_type=jnp.float32)
        score = score * DH ** (-0.5) + bias[...]
        top = jnp.max(score, axis=1, keepdims=True)
        weight = jnp.exp(score - top)
        total = jnp.sum(weight, axis=1, keepdims=True)
        out = jnp.dot(weight.astype(jnp.bfloat16), kv[1], preferred_element_type=jnp.float32)
        out = (out / total).astype(jnp.bfloat16)
        lse = top + jnp.log(total)
        for b in range(2):
            g = 2 * i + b
            part = slice(b * span, (b + 1) * span)
            soft_v[:, g * DH : (g + 1) * DH] = out[part]
            lse_v[g : g + 1, :] = jnp.sum(
                jnp.where(eye_s, lse[part], 0.0), axis=0, keepdims=True
            )
        pair = slice(2 * i * DH, 2 * (i + 1) * DH)
        stores.append(
            pltpu.make_async_copy(soft_v.at[:, pair], soft_out.at[:, pair], loc_sem.at[10 + i])
        )
        stores[-1].start()
    stores.append(pltpu.make_async_copy(lse_v, lse_out, loc_sem.at[10 + heads // 2]))
    stores[-1].start()

    for copy in kv1 + auxc + linc + qsc:
        copy.wait_send()
    for copy, peer in zip(kv2, seq_peers):
        pl.when(peer > me)(copy.wait_send)
    for block in range(n):
        pl.when(block != me)(result_to(block).wait_send)
    for source in range(n):
        arrived(out_from, source)
    own_out.wait()
    for copy in stores:
        copy.wait()


def fused(n, m, query_lin, key_lin, value_lin, log_decay, query_soft, key_soft, value_soft, doc_start):
    span, heads = query_lin.shape[0], log_decay.shape[0]
    tokens, rows = n * span, query_soft.shape[0]
    bf16, f32 = jnp.bfloat16, jnp.float32
    any_spec = pl.BlockSpec(memory_space=pl.ANY)
    hbm_spec = pl.BlockSpec(memory_space=pltpu.HBM)
    dma = pltpu.SemaphoreType.DMA
    results = pl.pallas_call(
        functools.partial(fused_kernel, n, m),
        out_shape=(
            jax.ShapeDtypeStruct((span, heads * DH), bf16),
            jax.ShapeDtypeStruct((span, heads * DH), bf16),
            jax.ShapeDtypeStruct((heads, span), f32),
        ),
        in_specs=[any_spec] * 8,
        out_specs=(any_spec,) * 3,
        scratch_shapes=[
            pltpu.VMEM((3, span, heads * DH), bf16),
            pltpu.VMEM((3, tokens, DH), bf16),
            pltpu.VMEM((2 * heads, DH), f32),
            pltpu.VMEM((n, 2 * heads, DH), f32),
            pltpu.VMEM((heads, span), f32),
            pltpu.VMEM((1, span), jnp.int32),
            pltpu.VMEM((span, heads * DH), bf16),
            pltpu.VMEM((2, rows, m * DH), bf16),
            pltpu.VMEM((2, tokens, DH), bf16),
            pltpu.VMEM((tokens, DH), bf16),
            pltpu.VMEM((span, heads * DH), bf16),
            pltpu.VMEM((heads, span), f32),
            pltpu.VMEM((2 * span, tokens), f32),
            dma((11 + heads // 2,)),
        ]
        + [dma((n,))] * 4
        + [dma((m - 1,))] * 4
        + [dma((n,))] * 4,
        compiler_params=pltpu.CompilerParams(
            collective_id=0, has_side_effects=True, vmem_limit_bytes=32 * 1024 * 1024
        ),
    )(*(pltpu.with_memory_space_constraint(x, pltpu.HBM) for x in (
        query_lin, key_lin, value_lin, log_decay, query_soft, key_soft, value_soft,
        doc_start.reshape(1, span),
    )))
    return pl.pallas_call(
        store_kernel,
        out_shape=tuple(jax.ShapeDtypeStruct(part.shape, part.dtype) for part in results),
        in_specs=[any_spec] * 3,
        out_specs=(hbm_spec,) * 3,
        scratch_shapes=[dma((3,))],
    )(*(pltpu.with_memory_space_constraint(part, pltpu.VMEM) for part in results))


def store_kernel(a, b, c, a_out, b_out, c_out, sem):
    copies = [
        pltpu.make_async_copy(src, dst, sem.at[i])
        for i, (src, dst) in enumerate(((a, a_out), (b, b_out), (c, c_out)))
    ]
    for copy in copies:
        copy.start()
    for copy in copies:
        copy.wait()


def per_device(
    query_lin, key_lin, value_lin, log_decay, query_soft, key_soft, value_soft, doc_start
):
    n, m = lax.axis_size("seq"), lax.axis_size("head")
    span, heads = query_lin.shape[0], log_decay.shape[0]
    if heads == n == 8 and span == DH // 2 and key_soft.shape[1] == m * DH:
        return fused(
            n, m, query_lin, key_lin, value_lin, log_decay,
            query_soft, key_soft, value_soft, doc_start,
        )
    lin_out = lightning_part(query_lin, key_lin, value_lin, log_decay, doc_start)
    soft_out, soft_lse = softmax_part(query_soft, key_soft, value_soft, doc_start)
    return (lin_out, soft_out, soft_lse)


def solution(mesh):
    return jax.shard_map(
        per_device,
        mesh=mesh,
        in_specs=(
            P("seq", "head"),
            P("seq", "head"),
            P("seq", "head"),
            P("head", "seq"),
            P(("seq", "head"), None),
            P(("seq", "head"), None),
            P(("seq", "head"), None),
            P("seq"),
        ),
        out_specs=(P("seq", "head"), P("seq", "head"), P("head", "seq")),
        check_vma=False,
    )
```
